32 devices in a mesh: dp: 8 (over z, y), tensor: 4 (over x, core).
Axes of the slice: x: 2, y: 2, z: 4, core: 2. Of those that a mesh axis runs over, the one named last changes fastest.
Arguments:
- tokens: bfloat16 [8192, 768], P(('dp', 'tensor')), may hold values from -6 to 6
- lengths: int32 [16], P('dp'), may hold values from 1 to 512, 4096 in all
- query_weight: bfloat16 [768, 768], P('dp', 'tensor'), may hold values from -0.3125 to 0.3125
- key_weight: bfloat16 [768, 768], P('dp', 'tensor'), may hold values from -0.3125 to 0.3125
- value_weight: bfloat16 [768, 768], P('dp', 'tensor'), may hold values from -0.21875 to 0.21875
- output_weight: bfloat16 [768, 768], P('tensor', 'dp'), may hold values from -1.25 to 1.25
- inner_weight: bfloat16 [768, 3072], P('dp', 'tensor'), may hold values from -0.21875 to 0.21875
- outer_weight: bfloat16 [3072, 768], P('tensor', 'dp'), may hold values from -0.15625 to 0.15625
- attn_down: bfloat16 [768, 64], replicated, may hold values from -0.21875 to 0.21875
- attn_down_bias: float32 [64], replicated, may hold values from -3 to 3
- attn_up: bfloat16 [64, 768], replicated, may hold values from -0.75 to 0.75
- attn_up_bias: float32 [768], replicated, may hold values from -3 to 3
- attn_norm_gain: float32 [768], replicated, may hold values from 0.5 to 1.5
- attn_norm_bias: float32 [768], replicated, may hold values from -2 to 2
- feed_down: bfloat16 [768, 64], replicated, may hold values from -0.21875 to 0.21875
- feed_down_bias: float32 [64], replicated, may hold values from -3 to 3
- feed_up: bfloat16 [64, 768], replicated, may hold values from -0.75 to 0.75
- feed_up_bias: float32 [768], replicated, may hold values from -3 to 3
- feed_norm_gain: float32 [768], replicated, may hold values from 0.5 to 1.5
- feed_norm_bias: float32 [768], replicated, may hold values from -2 to 2
- upstream: bfloat16 [8192, 768], P(('dp', 'tensor')), may hold values from -6 to 6
Outputs:
- layer_out: bfloat16 [8192, 768], P(('dp', 'tensor'))
- tokens_grad: bfloat16 [8192, 768], P(('dp', 'tensor'))
- attn_down_grad: float32 [768, 64], replicated
- attn_down_bias_grad: float32 [64], replicated
- attn_up_grad: float32 [64, 768], replicated
- attn_up_bias_grad: float32 [768], replicated
- attn_gain_grad: float32 [768], replicated
- attn_shift_grad: float32 [768], replicated
- feed_down_grad: float32 [768, 64], replicated
- feed_down_bias_grad: float32 [64], replicated
- feed_up_grad: float32 [64, 768], replicated
- feed_up_bias_grad: float32 [768], replicated
- feed_gain_grad: float32 [768], replicated
- feed_shift_grad: float32 [768], replicated
The draws below stay inside these ranges and needn't reach their ends.
Inputs may be any that keep to these rules, and one draw needn't show every extreme that they name: Sequence s has lengths[s] true tokens; its later positions are padding. The longest sequence has exactly 512 true tokens.
All inputs are finite; a program needn't handle non-finite values. No bound on the sum of `lengths` on one device may be relied on, other than what follows from the above.
Results may differ from the reference program's by a relative error of at most 0.025.
Values may be sent and summed in bfloat16 or wider, within the bound.
No kernel may reach another device: no remote copies, remote signals or barrier semaphores. Data moves between devices by JAX's collectives and lax.ppermute only.
A program may use at most 64 MiB of HBM per device.

```python
import math
import jax
import jax.numpy as jnp
import numpy as np
from jax import lax

D = 768
H = 12
HD = 64
FF = 3072
ADAPT = 64
L = 512
SEQ_DEV = 2
SEQS = 16
TOKENS = 8192


def block_scale(rng, dims, pieces, low, high):
    def one(axis_at, shards_of):
        steps = jax.random.uniform(jax.random.fold_in(jax.random.fold_in(rng, 6), axis_at), (shards_of,), jnp.float32, low / len(pieces), high / len(pieces))
        return jnp.repeat(jnp.exp(steps), dims[axis_at] // shards_of).reshape((-1,) + (1,) * (len(dims) - axis_at - 1))

    factor_of = one(*pieces[0])
    for cut in pieces[1:]:
        factor_of = factor_of * one(*cut)
    return factor_of


def profile(count, total, limit, lean):
    loads = [(1 << 20) // math.isqrt(standing ** lean) + 1 for standing in range(2, count + 1)]
    surplus, holding = total - limit - (count - 1), [1] * (count - 1)
    while surplus > 0:
        candidates = [i for i in range(count - 1) if holding[i] < limit]
        whole, remaining = sum([loads[i] for i in candidates]), surplus
        for i in candidates:
            addition = min(limit - holding[i], max(1, remaining * loads[i] // whole), surplus)
            holding[i] = holding[i] + addition
            surplus = surplus - addition
    return np.array([limit] + holding)


def ragged_sizes(key, amount, total, bound, skew):
    if amount == 2:
        one = jax.random.randint(key, (), max(1, total - bound), min(bound, total - 1) + 1)
        return jnp.stack([one, total - one])
    sizes = jnp.asarray(profile(amount, total, bound, skew), jnp.int32)
    couples = (amount - 1) // 2
    source_of, receiver = sizes[1:1 + 2 * couples:2], sizes[2:2 + 2 * couples:2]
    slack = jnp.minimum(source_of - 1, bound - receiver)
    passed = jax.random.randint(jax.random.fold_in(key, 1), (couples,), 0, 1 << 20) % (slack + 1)
    sizes = sizes.at[1:1 + 2 * couples:2].set(source_of - passed).at[2:2 + 2 * couples:2].set(receiver + passed)
    return sizes[jax.random.permutation(jax.random.fold_in(key, 2), amount)]


def scatter_about(own_key, shape, scale, limit, cuts=(), held_as=jnp.bfloat16):
    values = scale * jax.random.normal(own_key, shape, jnp.float32)
    if cuts:
        values = values * block_scale(own_key, shape, cuts, -0.22, 0.18)
    return jnp.clip(values, -limit, limit).astype(held_as)


def setup_inputs(seed: int = 0) -> dict:
    arg_keys = jax.random.split(jax.random.key(seed), 22)
    return {
        "tokens": scatter_about(arg_keys[0], (TOKENS, D), 1.0, 6.0, ((0, 32),)),
        "lengths": ragged_sizes(arg_keys[1], SEQS, SEQS * L // 2, L, 1).astype(jnp.int32),
        "query_weight": scatter_about(arg_keys[2], (D, D), (D // 2) ** -0.5, 0.3125, ((0, 8), (1, 4))),
        "key_weight": scatter_about(arg_keys[3], (D, D), (D // 2) ** -0.5, 0.3125, ((0, 8), (1, 4))),
        "value_weight": scatter_about(arg_keys[4], (D, D), D ** -0.5, 0.21875, ((0, 8), (1, 4))),
        "output_weight": scatter_about(arg_keys[5], (D, D), (D // 32) ** -0.5, 1.25, ((0, 4), (1, 8))),
        "inner_weight": scatter_about(arg_keys[6], (D, FF), D ** -0.5, 0.21875, ((0, 8), (1, 4))),
        "outer_weight": scatter_about(arg_keys[7], (FF, D), (FF // 2) ** -0.5, 0.15625, ((0, 4), (1, 8))),
        "attn_down": scatter_about(arg_keys[8], (D, ADAPT), D ** -0.5, 0.21875),
        "attn_down_bias": scatter_about(arg_keys[9], (ADAPT,), 0.5, 3.0, (), jnp.float32),
        "attn_up": scatter_about(arg_keys[10], (ADAPT, D), ADAPT ** -0.5, 0.75),
        "attn_up_bias": scatter_about(arg_keys[11], (D,), 0.5, 3.0, (), jnp.float32),
        "attn_norm_gain": jnp.clip(1.0 + 0.1 * jax.random.normal(arg_keys[12], (D,), jnp.float32), 0.5, 1.5),
        "attn_norm_bias": scatter_about(arg_keys[13], (D,), 0.3, 2.0, (), jnp.float32),
        "feed_down": scatter_about(arg_keys[14], (D, ADAPT), D ** -0.5, 0.21875),
        "feed_down_bias": scatter_about(arg_keys[15], (ADAPT,), 0.5, 3.0, (), jnp.float32),
        "feed_up": scatter_about(arg_keys[16], (ADAPT, D), ADAPT ** -0.5, 0.75),
        "feed_up_bias": scatter_about(arg_keys[17], (D,), 0.5, 3.0, (), jnp.float32),
        "feed_norm_gain": jnp.clip(1.0 + 0.1 * jax.random.normal(arg_keys[18], (D,), jnp.float32), 0.5, 1.5),
        "feed_norm_bias": scatter_about(arg_keys[19], (D,), 0.3, 2.0, (), jnp.float32),
        "upstream": scatter_about(arg_keys[20], (TOKENS, D), 1.0, 6.0, ((0, 32),)),
    }


@jax.custom_vjp
def low(v):
    return lax.optimization_barrier(v.astype(jnp.bfloat16)).astype(jnp.float32)

@jax.custom_vjp
def low_back(v):
    return v

def low_keep(v):
    return (low(v), None)

def low_pass(kept, grad):
    return (grad,)

def back_keep(v):
    return (v, None)

def back_low(kept, grad):
    return (low(grad),)
low.defvjp(low_keep, low_pass)
low_back.defvjp(back_keep, back_low)
EPSILON = 1e-05
MASKED = -1e+30

def matmul(left, right):
    return jnp.dot(left, right, precision=lax.Precision.HIGHEST, preferred_element_type=jnp.float32)

def norm_rows(summed, gain, shift):
    center = summed - lax.optimization_barrier(jnp.mean(summed, axis=-1, keepdims=True))
    spread = lax.optimization_barrier(jnp.mean(center * center, axis=-1, keepdims=True))
    return center * lax.rsqrt(spread + EPSILON) * gain + shift

def adapter(branch, down_weight, down_bias, up_weight, up_bias):
    preact = low_back(matmul(branch, down_weight) + down_bias)
    hidden = low(jax.nn.gelu(preact, approximate=False))
    return branch + low_back(matmul(hidden, up_weight)) + up_bias

def layer_forward(tokens_f, lengths, frozen, trained):
    query_w, key_w, value_w, output_w, inner_w, outer_w = frozen
    attn_down, attn_dbias, attn_up, attn_ubias, attn_gain, attn_shift, feed_down, feed_dbias, feed_up, feed_ubias, feed_gain, feed_shift = trained
    row_total = tokens_f.shape[0]
    seq_count = row_total // L

    def project(weight):
        return low(low_back(matmul(tokens_f, weight))).reshape(seq_count, L, H, HD)
    queries = project(query_w)
    keys_all = project(key_w)
    values_all = project(value_w)
    scores = jnp.einsum('sqhd,skhd->shqk', queries, keys_all, precision=lax.Precision.HIGHEST) * (1.0 / math.sqrt(HD))
    scores = low_back(scores)
    visible = jnp.arange(L)[None, :] < lengths[:, None]
    scores = jnp.where(visible[:, None, None, :], scores, MASKED)
    attn_probs = low(jax.nn.softmax(scores, axis=-1))
    context = jnp.einsum('shqk,skhd->sqhd', attn_probs, values_all, precision=lax.Precision.HIGHEST)
    context = low(low_back(context.reshape(row_total, H * HD)))
    attn_branch = low(low_back(matmul(context, output_w)))
    first_sum = tokens_f + adapter(attn_branch, attn_down, attn_dbias, attn_up, attn_ubias)
    middle = low(norm_rows(first_sum, attn_gain, attn_shift))
    inner_pre = low_back(matmul(middle, inner_w))
    inner_act = low(jax.nn.gelu(inner_pre, approximate=False))
    feed_branch = low(low_back(matmul(inner_act, outer_w)))
    second_sum = middle + adapter(feed_branch, feed_down, feed_dbias, feed_up, feed_ubias)
    return norm_rows(second_sum, feed_gain, feed_shift)

def reference(tokens, lengths, query_weight, key_weight, value_weight, output_weight, inner_weight, outer_weight, attn_down, attn_down_bias, attn_up, attn_up_bias, attn_norm_gain, attn_norm_bias, feed_down, feed_down_bias, feed_up, feed_up_bias, feed_norm_gain, feed_norm_bias, upstream):
    frozen = tuple((weight.astype(jnp.float32) for weight in (query_weight, key_weight, value_weight, output_weight, inner_weight, outer_weight)))
    trained = tuple((param.astype(jnp.float32) for param in (attn_down, attn_down_bias, attn_up, attn_up_bias, attn_norm_gain, attn_norm_bias, feed_down, feed_down_bias, feed_up, feed_up_bias, feed_norm_gain, feed_norm_bias)))
    group_rows = SEQ_DEV * L
    groups = tokens.shape[0] // group_rows
    token_blocks = tokens.astype(jnp.float32).reshape(groups, group_rows, D)
    length_blocks = lengths.reshape(groups, SEQ_DEV)
    upstream_blocks = upstream.astype(jnp.float32).reshape(groups, group_rows, D)

    def step(totals, item):
        block_tokens, block_lengths, block_upstream = item

        def run_layer(tokens_in, params_in):
            return layer_forward(tokens_in, block_lengths, frozen, params_in)
        result, pullback = jax.vjp(run_layer, block_tokens, trained)
        tokens_back, params_back = pullback(block_upstream)
        totals = jax.tree.map(jnp.add, totals, params_back)
        return (totals, (result.astype(jnp.bfloat16), tokens_back.astype(jnp.bfloat16)))
    zeros = tuple((jnp.zeros_like(param) for param in trained))
    totals, (results, tokens_back) = lax.scan(step, zeros, (token_blocks, length_blocks, upstream_blocks))
    factor = 1.0 / math.sqrt(TOKENS)
    grads = tuple((total * factor for total in totals))
    return (results.reshape(TOKENS, D), tokens_back.reshape(TOKENS, D), grads[0], grads[1], grads[2], grads[3], grads[4], grads[5], grads[6], grads[7], grads[8], grads[9], grads[10], grads[11])
```

```python
import math

import jax
import jax.numpy as jnp
from jax import lax
from jax.experimental import pallas as pl
from jax.experimental.pallas import tpu as pltpu
from jax.sharding import PartitionSpec as P

HD = 64
EPSILON = 1e-05
MASKED = -1e30
GROUP = 128
BF = jnp.bfloat16
F32 = jnp.float32
AXES = ("dp", "tensor")
GRAD_ROWS = 160


def nn(a, b):
    return lax.dot_general(a, b, (((1,), (0,)), ((), ())), preferred_element_type=F32)


def nt(a, b):
    return lax.dot_general(a, b, (((1,), (1,)), ((), ())), preferred_element_type=F32)


def tn(a, b):
    return lax.dot_general(a, b, (((0,), (0,)), ((), ())), preferred_element_type=F32)


def cdf_of(v):
    return 0.5 * (1.0 + lax.erf(v * (1.0 / math.sqrt(2.0))))


def gelu_slope(v, cdf):
    return cdf + v * (jnp.exp(-0.5 * v * v) * (1.0 / math.sqrt(2.0 * math.pi)))


class Staged:
    def __init__(self, plan, refs, rows_ref, dest, sems):
        self.copies = [[] for _ in range(4)]
        i = 0
        for ref, (slot, entries) in zip(refs, plan):
            n = len(entries)
            step = ref.shape[0] // n
            for j, e in enumerate(entries):
                row = pl.multiple_of(rows_ref[e], 32)
                self.copies[slot].append(
                    pltpu.make_async_copy(
                        ref.at[pl.ds(j * step, step), :],
                        dest.at[slot, pl.ds(row, step), :],
                        sems.at[i],
                    )
                )
                i += 1

    def start(self):
        for slot in self.copies:
            for c in slot:
                c.start()

    def wait(self, slot):
        for c in self.copies[slot]:
            c.wait()


def copies_of(plan):
    return sum(len(entries) for _, entries in plan)


def lane_low(rows):
    return lax.broadcasted_iota(jnp.int32, (rows, GROUP), 1) < HD


def stack_heads(pair):
    low = lane_low(pair.shape[0])
    zero = jnp.zeros_like(pair)
    return jnp.concatenate([jnp.where(low, pair, zero), jnp.where(low, zero, pair)], axis=0)


def swap_halves(v):
    return jnp.concatenate([v[:, HD:], v[:, :HD]], axis=1)


def front_kernel(plan, rows):
    pieces = len(plan)

    def body(rows_ref, info_ref, own_ref, other_ref, *refs):
        a_refs = refs[:pieces]
        (down, dbias, up, ubias, gain, shift) = refs[pieces : pieces + 6]
        (proj, probs2, probs1, branch_o, pre_o, mid_o, normed_o, inv_o) = refs[pieces + 6 : pieces + 14]
        (w, sems) = refs[pieces + 14 :]
        staged = Staged(plan, a_refs, rows_ref, w, sems)
        staged.start()
        length = info_ref[0]
        half = info_ref[1]
        at = lax.broadcasted_iota(jnp.int32, (1, 2 * rows), 1)
        place = jnp.where(at < rows, at + half * rows, at - rows + (1 - half) * rows)
        visible = place < length
        low = lane_low(rows)

        def softmax(raw):
            s = jnp.where(visible, raw * (1.0 / math.sqrt(HD)), MASKED)
            e = jnp.exp(s - jnp.max(s, axis=1, keepdims=True))
            return (e / jnp.sum(e, axis=1, keepdims=True)).astype(BF)

        branch = jnp.zeros((rows, own_ref.shape[1]), F32)
        for t in range(4):
            staged.wait(t)
            proj[t, 0:rows, :] = nn(own_ref[...], w[t, :, 0 : 5 * GROUP]).astype(BF)
            proj[t, rows : 2 * rows, GROUP : 5 * GROUP] = nn(
                other_ref[...], w[t, :, GROUP : 5 * GROUP]
            ).astype(BF)
            proj[t, rows : 2 * rows, 0:GROUP] = jnp.zeros((rows, GROUP), BF)
            p2 = softmax(nt(stack_heads(proj[t, 0:rows, 0:GROUP]), proj[t, :, GROUP : 2 * GROUP]))
            probs2[t] = p2
            both = nn(p2, proj[t, :, 2 * GROUP : 3 * GROUP])
            pair = jnp.where(low, both[0:rows], both[rows:])
            qc = swap_halves(proj[t, 0:rows, 3 * GROUP : 4 * GROUP])
            qc = jnp.where(low, jnp.zeros_like(qc), qc)
            p1 = softmax(nt(qc, proj[t, :, 3 * GROUP : 4 * GROUP]))
            probs1[t] = p1
            single = swap_halves(nn(p1, proj[t, :, 4 * GROUP : 5 * GROUP]))
            single = jnp.where(low, 0.0, single)
            context = jnp.concatenate([single, pair], axis=1).astype(BF)
            branch = branch + nt(context, w[t, :, 4 * GROUP : 6 * GROUP])
        branch_low = branch.astype(BF)
        branch_o[...] = branch_low
        pre = nn(branch_low, down[...]) + dbias[...]
        pre_o[...] = pre
        hidden = (pre * cdf_of(pre)).astype(BF)
        total = own_ref[...].astype(F32) + (branch_low.astype(F32) + nn(hidden, up[...]) + ubias[...])
        center = total - jnp.mean(total, axis=1, keepdims=True)
        inverse = lax.rsqrt(jnp.mean(center * center, axis=1, keepdims=True) + EPSILON)
        normed = center * inverse
        normed_o[...] = normed
        inv_o[...] = inverse
        mid_o[...] = (normed * gain[...] + shift[...]).astype(BF)

    return body


def inner_kernel(plan, rows):
    pieces = len(plan)

    def body(rows_ref, mid_ref, *refs):
        b_refs = refs[:pieces]
        act_o, slope_o, w, sems = refs[pieces:]
        staged = Staged(plan, b_refs, rows_ref, w, sems)
        staged.start()
        for t in range(4):
            staged.wait(t)
            pre = nn(mid_ref[...], w[t])
            cdf = cdf_of(pre)
            act_o[t] = (pre * cdf).astype(BF)
            slope_o[t] = gelu_slope(pre, cdf).astype(BF)

    return body


def norm_back(incoming, normed, inverse, gain):
    gain_grad = jnp.sum(incoming * normed, axis=0, keepdims=True)
    shift_grad = jnp.sum(incoming, axis=0, keepdims=True)
    scaled = incoming * gain
    row_mean = jnp.mean(scaled, axis=1, keepdims=True)
    row_proj = jnp.mean(scaled * normed, axis=1, keepdims=True)
    return inverse * (scaled - row_mean - normed * row_proj), gain_grad, shift_grad


def adapter_back(grads, g, branch_low, pre, hidden, cdf, down, up, gain_grad, shift_grad):
    g_low = g.astype(BF)
    hidden_grad = nt(g_low, up)
    pre_low = (hidden_grad * gelu_slope(pre, cdf)).astype(BF)
    n = pre.shape[1]
    grads[...] = jnp.zeros_like(grads)
    grads[0:n, :] = tn(pre_low, branch_low)
    grads[n : 2 * n, :] = tn(hidden, g_low)
    grads[2 * n : 2 * n + 1, :] = jnp.sum(g, axis=0, keepdims=True)
    grads[2 * n + 1 : 2 * n + 2, :] = gain_grad
    grads[2 * n + 2 : 2 * n + 3, :] = shift_grad
    grads[2 * n + 3 : 2 * n + 4, 0:n] = jnp.sum(pre_low.astype(F32), axis=0, keepdims=True)
    return (g + nt(pre_low, down)).astype(BF)


def middle_kernel(plan, rows):
    pieces = len(plan)

    def body(rows_ref, info_ref, act_ref, slope_ref, mid_ref, upstream, branch_ref, pre_ref, normed_ref, inv_ref, *refs):
        b_refs = refs[:pieces]
        c_refs = refs[pieces : 2 * pieces]
        (fdown, fdbias, fup, fubias, fgain, fshift, adown, aup, again) = refs[2 * pieces : 2 * pieces + 9]
        (out_o, back_o, first_o, keep_o, send_o) = refs[2 * pieces + 9 : 2 * pieces + 14]
        (wb, wc, fgrads, agrads, semb, semc) = refs[2 * pieces + 14 :]
        staged_c = Staged(plan, c_refs, rows_ref, wc, semc)
        staged_b = Staged(plan, b_refs, rows_ref, wb, semb)
        staged_c.start()
        staged_b.start()
        branch = jnp.zeros((rows, mid_ref.shape[1]), F32)
        for t in range(4):
            staged_c.wait(t)
            branch = branch + nt(act_ref[t], wc[t])
        branch_low = branch.astype(BF)
        pre = nn(branch_low, fdown[...]) + fdbias[...]
        cdf = cdf_of(pre)
        hidden = (pre * cdf).astype(BF)
        total = mid_ref[...].astype(F32) + (branch_low.astype(F32) + nn(hidden, fup[...]) + fubias[...])
        center = total - jnp.mean(total, axis=1, keepdims=True)
        inverse = lax.rsqrt(jnp.mean(center * center, axis=1, keepdims=True) + EPSILON)
        normed = center * inverse
        out_o[...] = (normed * fgain[...] + fshift[...]).astype(BF)
        second, gain_grad, shift_grad = norm_back(upstream[...].astype(F32), normed, inverse, fgain[...])
        back = adapter_back(fgrads, second, branch_low, pre, hidden, cdf, fdown[...], fup[...], gain_grad, shift_grad)
        mid_grad = second
        for t in range(4):
            staged_b.wait(t)
            inner_low = (nn(back, wc[t]) * slope_ref[t].astype(F32)).astype(BF)
            mid_grad = mid_grad + nt(inner_low, wb[t])
        normed1 = normed_ref[...]
        first, gain_grad, shift_grad = norm_back(mid_grad, normed1, inv_ref[...], again[...])
        first_o[...] = first
        pre1 = pre_ref[...]
        cdf1 = cdf_of(pre1)
        hidden1 = (pre1 * cdf1).astype(BF)
        back_o[...] = adapter_back(
            agrads, first, branch_ref[...], pre1, hidden1, cdf1, adown[...], aup[...], gain_grad, shift_grad
        )
        is_zero = info_ref[1] == 0
        f_all = fgrads[...]
        a_all = agrads[...]
        keep_o[...] = jnp.where(is_zero, f_all, a_all)
        send_o[...] = jnp.where(is_zero, a_all, f_all).astype(BF)

    return body


def back_kernel(plan, rows):
    pieces = len(plan)
    scale = 1.0 / math.sqrt(HD)

    def body(rows_ref, back_ref, proj, probs2, probs1, first_ref, *refs):
        a_refs = refs[:pieces]
        (own_o, send_o) = refs[pieces : pieces + 2]
        (w, grad, sems) = refs[pieces + 2 :]
        staged = Staged(plan, a_refs, rows_ref, w, sems)
        staged.start()
        low = lane_low(rows)

        def score_grad(p, dp):
            pf = p.astype(F32)
            inner = jnp.sum(pf * dp, axis=1, keepdims=True)
            return (pf * (dp - inner)).astype(BF)

        own = first_ref[...]
        sent = jnp.zeros(own.shape, F32)
        for t in range(4):
            staged.wait(t)
            d_context = nn(back_ref[...], w[t, :, 4 * GROUP : 6 * GROUP]).astype(BF)
            d_pair = stack_heads(d_context[:, GROUP:])
            p2 = probs2[t]
            ds = score_grad(p2, nt(d_pair, proj[t, :, 2 * GROUP : 3 * GROUP]))
            grad[:, 2 * GROUP : 3 * GROUP] = tn(p2, d_pair).astype(BF)
            grad[:, GROUP : 2 * GROUP] = (tn(ds, stack_heads(proj[t, 0:rows, 0:GROUP])) * scale).astype(BF)
            both = nn(ds, proj[t, :, GROUP : 2 * GROUP]) * scale
            grad[0:rows, 0:GROUP] = jnp.where(low, both[0:rows], both[rows:]).astype(BF)
            d_single = swap_halves(d_context[:, 0:GROUP])
            d_single = jnp.where(low, d_single, jnp.zeros_like(d_single))
            p1 = probs1[t]
            ds1 = score_grad(p1, nt(d_single, proj[t, :, 4 * GROUP : 5 * GROUP]))
            grad[:, 4 * GROUP : 5 * GROUP] = tn(p1, d_single).astype(BF)
            qc = swap_halves(proj[t, 0:rows, 3 * GROUP : 4 * GROUP])
            qc = jnp.where(low, jnp.zeros_like(qc), qc)
            dk = tn(ds1, qc) * scale
            dq = swap_halves(nn(ds1, proj[t, :, 3 * GROUP : 4 * GROUP])) * scale
            grad[0:rows, 3 * GROUP : 4 * GROUP] = jnp.where(low, dq, dk[0:rows]).astype(BF)
            grad[rows : 2 * rows, 3 * GROUP : 4 * GROUP] = dk[rows:].astype(BF)
            own = own + nt(grad[0:rows, :], w[t, :, 0 : 5 * GROUP])
            sent = sent + nt(grad[rows : 2 * rows, GROUP:], w[t, :, GROUP : 5 * GROUP])
        own_o[...] = own
        send_o[...] = sent.astype(BF)

    return body


VM = pl.BlockSpec(memory_space=pltpu.VMEM)
SM = pl.BlockSpec(memory_space=pltpu.SMEM)
ANY = pl.BlockSpec(memory_space=pl.ANY)


def call(body, name, in_specs, outs, scratch):
    return pl.pallas_call(
        body,
        name=name,
        in_specs=in_specs,
        out_specs=[VM] * len(outs),
        out_shape=[jax.ShapeDtypeStruct(s, d) for s, d in outs],
        scratch_shapes=scratch,
        compiler_params=pltpu.CompilerParams(vmem_limit_bytes=60000 * 1024),
    )


def pairs(step):
    out = []
    for d in range(8):
        for t in range(4):
            z, y, x, c = d // 2, d % 2, t // 2, t % 2
            z2, y2, x2, c2 = step(z, y, x, c)
            out.append((d * 4 + t, (z2 * 2 + y2) * 4 + x2 * 2 + c2))
    return out


CORE = pairs(lambda z, y, x, c: (z, y, x, 1 - c))
XDIR = pairs(lambda z, y, x, c: (z, y, 1 - x, c))
YDIR = pairs(lambda z, y, x, c: (z, 1 - y, x, c))
ZDIR = [None] + [pairs(lambda z, y, x, c, k=k: (z ^ k, y, x, c)) for k in (1, 2, 3)]
SPLIT1 = pairs(lambda z, y, x, c: (z, y, 1 - x, c) if c == 0 else (z, 1 - y, x, c))
SPLIT2 = pairs(lambda z, y, x, c: (z, 1 - y, x, c) if c == 0 else (z, y, 1 - x, c))


def pp(v, perm):
    return lax.ppermute(v, AXES, perm)


def fast_plan():
    plan = []
    for rc in range(2):
        plan += [
            (rc, [0, 1, 2, 3]),
            (2 + rc, [0, 1, 2, 3]),
            (rc, [4, 5, 6, 7]),
            (2 + rc, [4, 5]),
            (2 + rc, [6, 7]),
        ]
    return plan


def gather_fast(shard):
    n = shard.shape[0]
    line = jnp.concatenate([shard] + [pp(shard, ZDIR[k]) for k in (1, 2, 3)], axis=0)
    from_x = pp(line, XDIR)
    from_y = pp(line, YDIR)
    corner_x = pp(from_y[: 2 * n], XDIR)
    corner_y = pp(from_x[2 * n :], YDIR)
    mine = [line, from_x, from_y, corner_x, corner_y]
    return mine + [pp(v, CORE) for v in mine]


def gather_plain(shard):
    n = shard.shape[0]
    whole = lax.all_gather(shard, AXES, axis=0, tiled=False)
    whole = whole.reshape(lax.axis_size("dp"), lax.axis_size("tensor"), n, shard.shape[1])
    return [whole[:, t].reshape(-1, shard.shape[1]) for t in range(lax.axis_size("tensor"))]


def reduce_fast(keep, send, c, x, y):
    first = jnp.where(c == 0, x, y) == 1
    second = jnp.where(c == 0, y, x) == 1
    half = keep + pp(send, CORE).astype(F32)
    n = half.shape[0] // 2
    m = half.shape[1] // 2
    lo, hi = half[:n], half[n:]
    quarter = jnp.where(first, hi, lo) + pp(jnp.where(first, lo, hi).astype(BF), SPLIT1).astype(F32)
    lo, hi = quarter[:, :m], quarter[:, m:]
    part = jnp.where(second, hi, lo) + pp(jnp.where(second, lo, hi).astype(BF), SPLIT2).astype(F32)
    low = part.astype(BF)
    others = [pp(low, ZDIR[k]).astype(F32) for k in (1, 2, 3)]
    part = ((low.astype(F32) + others[0]) + (others[1] + others[2])).astype(BF)
    other = pp(part, SPLIT2)
    quarter = jnp.where(second, jnp.concatenate([other, part], 1), jnp.concatenate([part, other], 1))
    other = pp(quarter, SPLIT1)
    half = jnp.where(first, jnp.concatenate([other, quarter], 0), jnp.concatenate([quarter, other], 0))
    other = pp(half, CORE)
    return jnp.where(c == 0, half, other).astype(F32), jnp.where(c == 0, other, half).astype(F32)


def shards(
    tokens,
    lengths,
    query_weight,
    key_weight,
    value_weight,
    output_weight,
    inner_weight,
    outer_weight,
    attn_down,
    attn_down_bias,
    attn_up,
    attn_up_bias,
    attn_norm_gain,
    attn_norm_bias,
    feed_down,
    feed_down_bias,
    feed_up,
    feed_up_bias,
    feed_norm_gain,
    feed_norm_bias,
    upstream,
):
    dp_size, t_size = lax.axis_size("dp"), lax.axis_size("tensor")
    fast = dp_size == 8 and t_size == 4
    d = lax.axis_index("dp")
    t = lax.axis_index("tensor")
    rows, width = tokens.shape
    units = inner_weight.shape[1]
    n_adapt = attn_down.shape[1]

    partner = [(i * t_size + j, i * t_size + (j ^ 1)) for i in range(dp_size) for j in range(t_size)]
    other_tokens = pp(tokens, partner)

    out_t = output_weight.T
    q, k, v = query_weight, key_weight, value_weight
    pack_a = jnp.concatenate(
        [
            q[:, : 2 * HD],
            k[:, : 2 * HD],
            v[:, : 2 * HD],
            q[:, 2 * HD :],
            k[:, 2 * HD :],
            v[:, 2 * HD :],
            out_t[:, 2 * HD :],
            out_t[:, : 2 * HD],
        ],
        axis=1,
    )
    pack_c = outer_weight.T
    if fast:
        plan = fast_plan()
        a_pieces = gather_fast(pack_a)
        b_pieces = gather_fast(inner_weight)
        c_pieces = gather_fast(pack_c)
        z, y = d // 2, d % 2
        table = jnp.stack([((z ^ rz) * 2 + (y ^ ry)) * (width // 8) for ry in range(2) for rz in range(4)])
    else:
        plan = [(s, [0]) for s in range(4)]
        a_pieces, b_pieces, c_pieces = (gather_plain(s) for s in (pack_a, inner_weight, pack_c))
        table = jnp.zeros((8,), jnp.int32)
    table = table.astype(jnp.int32)
    count = copies_of(plan)
    half = t % 2
    info = jnp.stack([lengths[t // 2], half]).astype(jnp.int32)
    row = lambda vec: vec.reshape(1, -1)

    w_shape = pltpu.VMEM((4, width, width), BF)
    sem_shape = pltpu.SemaphoreType.DMA((count,))
    n_p = len(plan)

    proj, probs2, probs1, branch, pre, mid, normed, inv = call(
        front_kernel(plan, rows),
        "front",
        [SM, SM, VM, VM] + [ANY] * n_p + [VM] * 6,
        [
            ((4, 2 * rows, 5 * GROUP), BF),
            ((4, 2 * rows, 2 * rows), BF),
            ((4, rows, 2 * rows), BF),
            ((rows, width), BF),
            ((rows, n_adapt), F32),
            ((rows, width), BF),
            ((rows, width), F32),
            ((rows, 1), F32),
        ],
        [w_shape, sem_shape],
    )(
        table,
        info,
        tokens,
        other_tokens,
        *a_pieces,
        attn_down,
        row(attn_down_bias),
        attn_up,
        row(attn_up_bias),
        row(attn_norm_gain),
        row(attn_norm_bias),
    )

    act, slope = call(
        inner_kernel(plan, rows),
        "inner",
        [SM, VM] + [ANY] * n_p,
        [((4, rows, units), BF), ((4, rows, units), BF)],
        [w_shape, sem_shape],
    )(table, mid, *b_pieces)

    layer_out, attn_back, first, keep, send = call(
        middle_kernel(plan, rows),
        "middle",
        [SM, SM] + [VM] * 8 + [ANY] * (2 * n_p) + [VM] * 9,
        [
            ((rows, width), BF),
            ((rows, width), BF),
            ((rows, width), F32),
            ((GRAD_ROWS, width), F32),
            ((GRAD_ROWS, width), BF),
        ],
        [
            w_shape,
            w_shape,
            pltpu.VMEM((GRAD_ROWS, width), F32),
            pltpu.VMEM((GRAD_ROWS, width), F32),
            sem_shape,
            sem_shape,
        ],
    )(
        table,
        info,
        act,
        slope,
        mid,
        upstream,
        branch,
        pre,
        normed,
        inv,
        *b_pieces,
        *c_pieces,
        feed_down,
        row(feed_down_bias),
        feed_up,
        row(feed_up_bias),
        row(feed_norm_gain),
        row(feed_norm_bias),
        attn_down,
        attn_up,
        row(attn_norm_gain),
    )

    own, sent = call(
        back_kernel(plan, rows),
        "back",
        [SM, VM, VM, VM, VM, VM] + [ANY] * n_p,
        [((rows, width), F32), ((rows, width), BF)],
        [w_shape, pltpu.VMEM((2 * rows, 5 * GROUP), BF), sem_shape],
    )(table, attn_back, proj, probs2, probs1, first, *a_pieces)
    tokens_grad = (own + pp(sent, partner).astype(F32)).astype(BF)

    if fast:
        feed_g, attn_g = reduce_fast(keep, send, half, t // 2, d % 2)
    else:
        is_zero = half == 0
        sent32 = send.astype(F32)
        feed_g = lax.psum(jnp.where(is_zero, keep, sent32), AXES)
        attn_g = lax.psum(jnp.where(is_zero, sent32, keep), AXES)
    grad_scale = 1.0 / math.sqrt(rows * dp_size * t_size)

    def outputs(g):
        g = g * grad_scale
        n = n_adapt
        return [
            g[:n].T,
            g[2 * n + 3, :n],
            g[n : 2 * n],
            g[2 * n],
            g[2 * n + 1],
            g[2 * n + 2],
        ]

    return (layer_out, tokens_grad, *outputs(attn_g), *outputs(feed_g))


def solution(mesh):
    in_specs = (
        P(("dp", "tensor"), None),
        P("dp"),
        P("dp", "tensor"),
        P("dp", "tensor"),
        P("dp", "tensor"),
        P("tensor", "dp"),
        P("dp", "tensor"),
        P("tensor", "dp"),
        *([P()] * 12),
        P(("dp", "tensor"), None),
    )
    out_specs = (
        P(("dp", "tensor"), None),
        P(("dp", "tensor"), None),
        *([P()] * 12),
    )
    return jax.shard_map(shards, mesh=mesh, in_specs=in_specs, out_specs=out_specs, check_vma=False)
```

```python
import math

import jax
import jax.numpy as jnp
from jax import lax
from jax.experimental import pallas as pl
from jax.experimental.pallas import tpu as pltpu
from jax.sharding import PartitionSpec as P

HD = 64
EPSILON = 1e-05
MASKED = -1e30
GROUP = 128
BF = jnp.bfloat16
F32 = jnp.float32
AXES = ("dp", "tensor")
GRAD_ROWS = 160


def nn(a, b):
    return lax.dot_general(a, b, (((1,), (0,)), ((), ())), preferred_element_type=F32)


def nt(a, b):
    return lax.dot_general(a, b, (((1,), (1,)), ((), ())), preferred_element_type=F32)


def tn(a, b):
    return lax.dot_general(a, b, (((0,), (0,)), ((), ())), preferred_element_type=F32)


def cdf_of(v):
    return 0.5 * (1.0 + lax.erf(v * (1.0 / math.sqrt(2.0))))


def gelu_slope(v, cdf):
    return cdf + v * (jnp.exp(-0.5 * v * v) * (1.0 / math.sqrt(2.0 * math.pi)))


class Staged:
    def __init__(self, plan, refs, rows_ref, dest, sems):
        self.copies = [[] for _ in range(4)]
        i = 0
        for ref, (slot, entries) in zip(refs, plan):
            n = len(entries)
            step = ref.shape[0] // n
            for j, e in enumerate(entries):
                row = pl.multiple_of(rows_ref[e], 32)
                self.copies[slot].append(
                    pltpu.make_async_copy(
                        ref.at[pl.ds(j * step, step), :],
                        dest.at[slot, pl.ds(row, step), :],
                        sems.at[i],
                    )
                )
                i += 1

    def start(self):
        for slot in self.copies:
            for c in slot:
                c.start()

    def wait(self, slot):
        for c in self.copies[slot]:
            c.wait()


def copies_of(plan):
    return sum(len(entries) for _, entries in plan)


def lane_low(rows):
    return lax.broadcasted_iota(jnp.int32, (rows, GROUP), 1) < HD


def stack_heads(pair):
    low = lane_low(pair.shape[0])
    zero = jnp.zeros_like(pair)
    return jnp.concatenate([jnp.where(low, pair, zero), jnp.where(low, zero, pair)], axis=0)


def swap_halves(v):
    return jnp.concatenate([v[:, HD:], v[:, :HD]], axis=1)


def pack_kernel(q_ref, k_ref, v_ref, o_ref, out, wide):
    n = q_ref.shape[0]
    wide[...] = jnp.zeros_like(wide)
    wide[:, 0:n] = o_ref[...].astype(F32)
    turned = wide[...].T[0:n].astype(BF)
    for i, ref in enumerate((q_ref, k_ref, v_ref)):
        out[:, i * GROUP : (i + 1) * GROUP] = ref[:, 0:GROUP]
    out[:, 3 * GROUP : 4 * GROUP] = jnp.concatenate([q_ref[:, GROUP:], k_ref[:, GROUP:]], axis=1)
    out[:, 4 * GROUP : 5 * GROUP] = jnp.concatenate([v_ref[:, GROUP:], turned[:, GROUP:]], axis=1)
    out[:, 5 * GROUP :] = turned[:, 0:GROUP]


def front_kernel(plan, rows):
    pieces = len(plan)

    def body(rows_ref, info_ref, own_ref, other_ref, *refs):
        a_refs = refs[:pieces]
        (down, dbias, up, ubias, gain, shift) = refs[pieces : pieces + 6]
        outs = refs[pieces + 6 :]
        projs, probs2, probs1 = outs[0:4], outs[4:8], outs[8:12]
        (branch_o, pre_o, mid_o, normed_o, inv_o, w, sems) = outs[12:]
        staged = Staged(plan, a_refs, rows_ref, w, sems)
        staged.start()
        length = info_ref[0]
        half = info_ref[1]
        at = lax.broadcasted_iota(jnp.int32, (1, 2 * rows), 1)
        place = jnp.where(at < rows, at + half * rows, at - rows + (1 - half) * rows)
        visible = place < length
        low = lane_low(rows)

        def softmax(raw):
            s = jnp.where(visible, raw * (1.0 / math.sqrt(HD)), MASKED)
            e = jnp.exp(s - jnp.max(s, axis=1, keepdims=True))
            return (e / jnp.sum(e, axis=1, keepdims=True)).astype(BF)

        branch = jnp.zeros((rows, own_ref.shape[1]), F32)
        for t in range(4):
            staged.wait(t)
            proj = projs[t]
            proj[0:rows, :] = nn(own_ref[...], w[t, :, 0 : 5 * GROUP]).astype(BF)
            proj[rows : 2 * rows, GROUP : 5 * GROUP] = nn(
                other_ref[...], w[t, :, GROUP : 5 * GROUP]
            ).astype(BF)
            proj[rows : 2 * rows, 0:GROUP] = jnp.zeros((rows, GROUP), BF)
            p2 = softmax(nt(stack_heads(proj[0:rows, 0:GROUP]), proj[:, GROUP : 2 * GROUP]))
            probs2[t][...] = p2
            both = nn(p2, proj[:, 2 * GROUP : 3 * GROUP])
            pair = jnp.where(low, both[0:rows], both[rows:])
            qc = swap_halves(proj[0:rows, 3 * GROUP : 4 * GROUP])
            qc = jnp.where(low, jnp.zeros_like(qc), qc)
            p1 = softmax(nt(qc, proj[:, 3 * GROUP : 4 * GROUP]))
            probs1[t][...] = p1
            single = swap_halves(nn(p1, proj[:, 4 * GROUP : 5 * GROUP]))
            single = jnp.where(low, 0.0, single)
            context = jnp.concatenate([single, pair], axis=1).astype(BF)
            branch = branch + nt(context, w[t, :, 4 * GROUP : 6 * GROUP])
        branch_low = branch.astype(BF)
        branch_o[...] = branch_low
        pre = nn(branch_low, down[...]) + dbias[...]
        pre_o[...] = pre
        hidden = (pre * cdf_of(pre)).astype(BF)
        total = own_ref[...].astype(F32) + (branch_low.astype(F32) + nn(hidden, up[...]) + ubias[...])
        center = total - jnp.mean(total, axis=1, keepdims=True)
        inverse = lax.rsqrt(jnp.mean(center * center, axis=1, keepdims=True) + EPSILON)
        normed = center * inverse
        normed_o[...] = normed
        inv_o[...] = inverse
        mid_o[...] = (normed * gain[...] + shift[...]).astype(BF)

    return body


def inner_kernel(plan, rows):
    pieces = len(plan)

    def body(rows_ref, mid_ref, *refs):
        b_refs = refs[:pieces]
        act_o, slope_o, w, sems = refs[pieces:]
        staged = Staged(plan, b_refs, rows_ref, w, sems)
        staged.start()
        for t in range(4):
            staged.wait(t)
            pre = nn(mid_ref[...], w[t])
            cdf = cdf_of(pre)
            act_o[t] = (pre * cdf).astype(BF)
            slope_o[t] = gelu_slope(pre, cdf).astype(BF)

    return body


def norm_back(incoming, normed, inverse, gain):
    gain_grad = jnp.sum(incoming * normed, axis=0, keepdims=True)
    shift_grad = jnp.sum(incoming, axis=0, keepdims=True)
    scaled = incoming * gain
    row_mean = jnp.mean(scaled, axis=1, keepdims=True)
    row_proj = jnp.mean(scaled * normed, axis=1, keepdims=True)
    return inverse * (scaled - row_mean - normed * row_proj), gain_grad, shift_grad


def adapter_back(grads, g, branch_low, pre, hidden, cdf, down, up, gain_grad, shift_grad):
    g_low = g.astype(BF)
    hidden_grad = nt(g_low, up)
    pre_low = (hidden_grad * gelu_slope(pre, cdf)).astype(BF)
    n = pre.shape[1]
    grads[...] = jnp.zeros_like(grads)
    grads[0:n, :] = tn(pre_low, branch_low)
    grads[n : 2 * n, :] = tn(hidden, g_low)
    grads[2 * n : 2 * n + 1, :] = jnp.sum(g, axis=0, keepdims=True)
    grads[2 * n + 1 : 2 * n + 2, :] = gain_grad
    grads[2 * n + 2 : 2 * n + 3, :] = shift_grad
    grads[2 * n + 3 : 2 * n + 4, 0:n] = jnp.sum(pre_low.astype(F32), axis=0, keepdims=True)
    return (g + nt(pre_low, down)).astype(BF)


def middle_kernel(plan, rows):
    pieces = len(plan)

    def body(rows_ref, info_ref, act_ref, slope_ref, mid_ref, upstream, branch_ref, pre_ref, normed_ref, inv_ref, *refs):
        b_refs = refs[:pieces]
        c_refs = refs[pieces : 2 * pieces]
        (fdown, fdbias, fup, fubias, fgain, fshift, adown, aup, again) = refs[2 * pieces : 2 * pieces + 9]
        (out_o, back_o, first_o, keep_o, send_o) = refs[2 * pieces + 9 : 2 * pieces + 14]
        (wb, wc, fgrads, agrads, semb, semc) = refs[2 * pieces + 14 :]
        staged_c = Staged(plan, c_refs, rows_ref, wc, semc)
        staged_b = Staged(plan, b_refs, rows_ref, wb, semb)
        staged_c.start()
        staged_b.start()
        branch = jnp.zeros((rows, mid_ref.shape[1]), F32)
        for t in range(4):
            staged_c.wait(t)
            branch = branch + nt(act_ref[t], wc[t])
        branch_low = branch.astype(BF)
        pre = nn(branch_low, fdown[...]) + fdbias[...]
        cdf = cdf_of(pre)
        hidden = (pre * cdf).astype(BF)
        total = mid_ref[...].astype(F32) + (branch_low.astype(F32) + nn(hidden, fup[...]) + fubias[...])
        center = total - jnp.mean(total, axis=1, keepdims=True)
        inverse = lax.rsqrt(jnp.mean(center * center, axis=1, keepdims=True) + EPSILON)
        normed = center * inverse
        out_o[...] = (normed * fgain[...] + fshift[...]).astype(BF)
        second, gain_grad, shift_grad = norm_back(upstream[...].astype(F32), normed, inverse, fgain[...])
        back = adapter_back(fgrads, second, branch_low, pre, hidden, cdf, fdown[...], fup[...], gain_grad, shift_grad)
        mid_grad = second
        for t in range(4):
            staged_b.wait(t)
            inner_low = (nn(back, wc[t]) * slope_ref[t].astype(F32)).astype(BF)
            mid_grad = mid_grad + nt(inner_low, wb[t])
        normed1 = normed_ref[...]
        first, gain_grad, shift_grad = norm_back(mid_grad, normed1, inv_ref[...], again[...])
        first_o[...] = first
        pre1 = pre_ref[...]
        cdf1 = cdf_of(pre1)
        hidden1 = (pre1 * cdf1).astype(BF)
        back_o[...] = adapter_back(
            agrads, first, branch_ref[...], pre1, hidden1, cdf1, adown[...], aup[...], gain_grad, shift_grad
        )
        is_zero = info_ref[1] == 0
        f_all = fgrads[...]
        a_all = agrads[...]
        keep_o[...] = jnp.where(is_zero, f_all, a_all)
        send_o[...] = jnp.where(is_zero, a_all, f_all).astype(BF)

    return body


def back_kernel(plan, rows, t):
    pieces = len(plan)
    scale = 1.0 / math.sqrt(HD)

    def body(rows_ref, back_ref, proj, probs2, probs1, own_in, sent_in, *refs):
        a_refs = refs[:pieces]
        (own_o, sent_o) = refs[pieces : pieces + 2]
        (w, grad, sems) = refs[pieces + 2 :]
        staged = Staged(plan, a_refs, rows_ref, w, sems)
        staged.start()
        low = lane_low(rows)

        def score_grad(p, dp):
            pf = p.astype(F32)
            inner = jnp.sum(pf * dp, axis=1, keepdims=True)
            return (pf * (dp - inner)).astype(BF)

        staged.wait(0)
        d_context = nn(back_ref[...], w[0, :, 4 * GROUP : 6 * GROUP]).astype(BF)
        d_pair = stack_heads(d_context[:, GROUP:])
        p2 = probs2[...]
        ds = score_grad(p2, nt(d_pair, proj[:, 2 * GROUP : 3 * GROUP]))
        grad[:, 2 * GROUP : 3 * GROUP] = tn(p2, d_pair).astype(BF)
        grad[:, GROUP : 2 * GROUP] = (tn(ds, stack_heads(proj[0:rows, 0:GROUP])) * scale).astype(BF)
        both = nn(ds, proj[:, GROUP : 2 * GROUP]) * scale
        grad[0:rows, 0:GROUP] = jnp.where(low, both[0:rows], both[rows:]).astype(BF)
        d_single = swap_halves(d_context[:, 0:GROUP])
        d_single = jnp.where(low, d_single, jnp.zeros_like(d_single))
        p1 = probs1[...]
        ds1 = score_grad(p1, nt(d_single, proj[:, 4 * GROUP : 5 * GROUP]))
        grad[:, 4 * GROUP : 5 * GROUP] = tn(p1, d_single).astype(BF)
        qc = swap_halves(proj[0:rows, 3 * GROUP : 4 * GROUP])
        qc = jnp.where(low, jnp.zeros_like(qc), qc)
        dk = tn(ds1, qc) * scale
        dq = swap_halves(nn(ds1, proj[:, 3 * GROUP : 4 * GROUP])) * scale
        grad[0:rows, 3 * GROUP : 4 * GROUP] = jnp.where(low, dq, dk[0:rows]).astype(BF)
        grad[rows : 2 * rows, 3 * GROUP : 4 * GROUP] = dk[rows:].astype(BF)
        own_o[...] = own_in[...] + nt(grad[0:rows, :], w[0, :, 0 : 5 * GROUP])
        sent = nt(grad[rows : 2 * rows, GROUP:], w[0, :, GROUP : 5 * GROUP])
        sent_o[...] = (sent_in[...] + sent).astype(sent_o.dtype)

    return body


VM = pl.BlockSpec(memory_space=pltpu.VMEM)
SM = pl.BlockSpec(memory_space=pltpu.SMEM)
ANY = pl.BlockSpec(memory_space=pl.ANY)


def call(body, name, in_specs, outs, scratch, micros):
    return pl.pallas_call(
        body,
        name=name,
        in_specs=in_specs,
        out_specs=[VM] * len(outs),
        out_shape=[jax.ShapeDtypeStruct(s, d) for s, d in outs],
        scratch_shapes=scratch,
        cost_estimate=pl.CostEstimate(flops=int(micros * 1e9), transcendentals=0, bytes_accessed=1 << 20),
        compiler_params=pltpu.CompilerParams(vmem_limit_bytes=60000 * 1024),
    )


def pairs(step):
    out = []
    for d in range(8):
        for t in range(4):
            z, y, x, c = d // 2, d % 2, t // 2, t % 2
            z2, y2, x2, c2 = step(z, y, x, c)
            out.append((d * 4 + t, (z2 * 2 + y2) * 4 + x2 * 2 + c2))
    return out


CORE = pairs(lambda z, y, x, c: (z, y, x, 1 - c))
XDIR = pairs(lambda z, y, x, c: (z, y, 1 - x, c))
YDIR = pairs(lambda z, y, x, c: (z, 1 - y, x, c))
ZDIR = [None] + [pairs(lambda z, y, x, c, k=k: (z ^ k, y, x, c)) for k in (1, 2, 3)]
SPLIT1 = pairs(lambda z, y, x, c: (z, y, 1 - x, c) if c == 0 else (z, 1 - y, x, c))
SPLIT2 = pairs(lambda z, y, x, c: (z, 1 - y, x, c) if c == 0 else (z, y, 1 - x, c))


def pp(v, perm):
    return lax.ppermute(v, AXES, perm)


def fast_plan():
    plan = []
    for rc in range(2):
        plan += [
            (rc, [0, 1, 2, 3]),
            (2 + rc, [0, 1, 2, 3]),
            (rc, [4, 5, 6, 7]),
            (2 + rc, [4, 5]),
            (2 + rc, [6, 7]),
        ]
    return plan


def after(value, *others):
    return lax.optimization_barrier((value, *others))[0]


class Gather:
    def __init__(self, shard):
        self.shard = shard
        self.n = shard.shape[0]

    def depth(self):
        parts = [self.shard] + [pp(self.shard, ZDIR[k]) for k in (1, 2, 3)]
        self.line = jnp.concatenate(parts, axis=0)

    def plane(self):
        self.from_x = pp(self.line, XDIR)
        self.from_y = pp(self.line, YDIR)

    def corner(self):
        self.corner_x = pp(self.from_y[: 2 * self.n], XDIR)
        self.corner_y = pp(self.from_x[2 * self.n :], YDIR)

    def pieces(self):
        mine = [self.line, self.from_x, self.from_y, self.corner_x, self.corner_y]
        return mine + [pp(v, CORE) for v in mine]


class Gathers:
    def __init__(self, a, b, c, small):
        self.a, self.b, self.c = a, b, c = Gather(a), Gather(b), Gather(c)
        a.depth()
        a.line, *self.small = lax.optimization_barrier((a.line, *small))
        a.plane()
        b.shard = after(b.shard, a.line)
        b.depth()
        c.shard = after(c.shard, b.line)
        c.depth()
        a.corner()
        b.line = after(b.line, a.corner_x, a.corner_y)
        b.plane()

    def first(self):
        return self.a.pieces()

    def second(self, mid):
        b, c = self.b, self.c
        b.from_x, b.from_y, c.line, _ = lax.optimization_barrier((b.from_x, b.from_y, c.line, mid))
        b.corner()
        c.line = after(c.line, b.corner_x, b.corner_y)
        c.plane()
        return b.pieces()

    def third(self, act):
        c = self.c
        c.from_x, c.from_y, _ = lax.optimization_barrier((c.from_x, c.from_y, act))
        c.corner()
        return c.pieces()


def gather_plain(shard):
    n = shard.shape[0]
    whole = lax.all_gather(shard, AXES, axis=0, tiled=False)
    whole = whole.reshape(lax.axis_size("dp"), lax.axis_size("tensor"), n, shard.shape[1])
    return [whole[:, t].reshape(-1, shard.shape[1]) for t in range(lax.axis_size("tensor"))]


def reduce_fast(keep, send, c, x, y, steps):
    first = jnp.where(c == 0, x, y) == 1
    second = jnp.where(c == 0, y, x) == 1
    half = keep + after(pp(send, CORE), steps[0]).astype(F32)
    n = half.shape[0] // 2
    m = half.shape[1] // 2
    lo, hi = half[:n], half[n:]
    quarter = jnp.where(first, hi, lo) + after(
        pp(jnp.where(first, lo, hi).astype(BF), SPLIT1), steps[1]
    ).astype(F32)
    lo, hi = quarter[:, :m], quarter[:, m:]
    part = jnp.where(second, hi, lo) + after(
        pp(jnp.where(second, lo, hi).astype(BF), SPLIT2), steps[2]
    ).astype(F32)
    low = part.astype(BF)
    others = [after(pp(low, ZDIR[k]), steps[3]).astype(F32) for k in (1, 2, 3)]
    part = ((low.astype(F32) + others[0]) + (others[1] + others[2])).astype(BF)
    other = pp(part, SPLIT2)
    quarter = jnp.where(second, jnp.concatenate([other, part], 1), jnp.concatenate([part, other], 1))
    other = pp(quarter, SPLIT1)
    half = jnp.where(first, jnp.concatenate([other, quarter], 0), jnp.concatenate([quarter, other], 0))
    other = pp(half, CORE)
    return jnp.where(c == 0, half, other).astype(F32), jnp.where(c == 0, other, half).astype(F32)


def shards(
    tokens,
    lengths,
    query_weight,
    key_weight,
    value_weight,
    output_weight,
    inner_weight,
    outer_weight,
    attn_down,
    attn_down_bias,
    attn_up,
    attn_up_bias,
    attn_norm_gain,
    attn_norm_bias,
    feed_down,
    feed_down_bias,
    feed_up,
    feed_up_bias,
    feed_norm_gain,
    feed_norm_bias,
    upstream,
):
    dp_size, t_size = lax.axis_size("dp"), lax.axis_size("tensor")
    fast = dp_size == 8 and t_size == 4
    d = lax.axis_index("dp")
    t = lax.axis_index("tensor")
    rows, width = tokens.shape
    units = inner_weight.shape[1]
    n_adapt = attn_down.shape[1]

    partner = [(i * t_size + j, i * t_size + (j ^ 1)) for i in range(dp_size) for j in range(t_size)]
    other_tokens = pp(tokens, partner)

    pack_a = call(
        pack_kernel,
        "pack",
        [VM] * 4,
        [((query_weight.shape[0], 6 * GROUP), BF)],
        [pltpu.VMEM((3 * HD, GROUP), F32)],
        1,
    )(query_weight, key_weight, value_weight, output_weight)[0]
    pack_c = outer_weight.T
    if fast:
        plan = fast_plan()
        z, y = d // 2, d % 2
        table = jnp.stack([((z ^ rz) * 2 + (y ^ ry)) * (width // 8) for ry in range(2) for rz in range(4)])
    else:
        plan = [(s, [0]) for s in range(4)]
        a_pieces, b_pieces, c_pieces = (gather_plain(s) for s in (pack_a, inner_weight, pack_c))
        table = jnp.zeros((8,), jnp.int32)
    table = table.astype(jnp.int32)
    count = copies_of(plan)
    half = t % 2
    info = jnp.stack([lengths[t // 2], half]).astype(jnp.int32)
    vectors = (
        attn_down_bias,
        attn_up_bias,
        attn_norm_gain,
        attn_norm_bias,
        feed_down_bias,
        feed_up_bias,
        feed_norm_gain,
        feed_norm_bias,
    )
    small = [table, info, attn_down, attn_up, feed_down, feed_up] + [v.reshape(1, -1) for v in vectors]
    if fast:
        gathers = Gathers(pack_a, inner_weight, pack_c, small)
        small = gathers.small
        a_pieces = gathers.first()
    (table, info, attn_down, attn_up, feed_down, feed_up, a_dbias, a_ubias, a_gain, a_shift, f_dbias, f_ubias, f_gain, f_shift) = small

    w_shape = pltpu.VMEM((4, width, width), BF)
    sem_shape = pltpu.SemaphoreType.DMA((count,))
    n_p = len(plan)

    *heads, branch, pre, mid, normed, inv = call(
        front_kernel(plan, rows),
        "front",
        [SM, SM, VM, VM] + [ANY] * n_p + [VM] * 6,
        [
            *([((2 * rows, 5 * GROUP), BF)] * 4),
            *([((2 * rows, 2 * rows), BF)] * 4),
            *([((rows, 2 * rows), BF)] * 4),
            ((rows, width), BF),
            ((rows, n_adapt), F32),
            ((rows, width), BF),
            ((rows, width), F32),
            ((rows, 1), F32),
        ],
        [w_shape, sem_shape],
        12,
    )(
        table,
        info,
        tokens,
        other_tokens,
        *a_pieces,
        attn_down,
        a_dbias,
        attn_up,
        a_ubias,
        a_gain,
        a_shift,
    )

    if fast:
        b_pieces = gathers.second(mid)
    act, slope = call(
        inner_kernel(plan, rows),
        "inner",
        [SM, VM] + [ANY] * n_p,
        [((4, rows, units), BF), ((4, rows, units), BF)],
        [w_shape, sem_shape],
        7,
    )(table, mid, *b_pieces)

    if fast:
        c_pieces = gathers.third(act)
    layer_out, attn_back, first, keep, send = call(
        middle_kernel(plan, rows),
        "middle",
        [SM, SM] + [VM] * 8 + [ANY] * (2 * n_p) + [VM] * 9,
        [
            ((rows, width), BF),
            ((rows, width), BF),
            ((rows, width), F32),
            ((GRAD_ROWS, width), F32),
            ((GRAD_ROWS, width), BF),
        ],
        [
            w_shape,
            w_shape,
            pltpu.VMEM((GRAD_ROWS, width), F32),
            pltpu.VMEM((GRAD_ROWS, width), F32),
            sem_shape,
            sem_shape,
        ],
        15,
    )(
        table,
        info,
        act,
        slope,
        mid,
        upstream,
        branch,
        pre,
        normed,
        inv,
        *b_pieces,
        *c_pieces,
        feed_down,
        f_dbias,
        feed_up,
        f_ubias,
        f_gain,
        f_shift,
        attn_down,
        attn_up,
        a_gain,
    )

    own, sent, steps = first, jnp.zeros((rows, width), F32), []
    for slot in range(4):
        chosen = [i for i, (at, _) in enumerate(plan) if at == slot]
        own_plan = [(0, plan[i][1]) for i in chosen]
        own, sent = call(
            back_kernel(own_plan, rows, slot),
            f"back{slot}",
            [SM] + [VM] * 6 + [ANY] * len(chosen),
            [((rows, width), F32), ((rows, width), F32 if slot < 3 else BF)],
            [
                pltpu.VMEM((1, width, width), BF),
                pltpu.VMEM((2 * rows, 5 * GROUP), BF),
                pltpu.SemaphoreType.DMA((copies_of(own_plan),)),
            ],
            4,
        )(
            table,
            attn_back,
            heads[slot],
            heads[4 + slot],
            heads[8 + slot],
            own,
            sent,
            *[a_pieces[i] for i in chosen],
        )
        steps.append(own)
    tokens_grad = (own + pp(sent, partner).astype(F32)).astype(BF)

    if fast:
        feed_g, attn_g = reduce_fast(keep, send, half, t // 2, d % 2, steps)
    else:
        is_zero = half == 0
        sent32 = send.astype(F32)
        feed_g = lax.psum(jnp.where(is_zero, keep, sent32), AXES)
        attn_g = lax.psum(jnp.where(is_zero, sent32, keep), AXES)
    grad_scale = 1.0 / math.sqrt(rows * dp_size * t_size)

    def outputs(g):
        g = g * grad_scale
        n = n_adapt
        return [
            g[:n].T,
            g[2 * n + 3, :n],
            g[n : 2 * n],
            g[2 * n],
            g[2 * n + 1],
            g[2 * n + 2],
        ]

    return (layer_out, tokens_grad, *outputs(attn_g), *outputs(feed_g))


def solution(mesh):
    in_specs = (
        P(("dp", "tensor"), None),
        P("dp"),
        P("dp", "tensor"),
        P("dp", "tensor"),
        P("dp", "tensor"),
        P("tensor", "dp"),
        P("dp", "tensor"),
        P("tensor", "dp"),
        *([P()] * 12),
        P(("dp", "tensor"), None),
    )
    out_specs = (
        P(("dp", "tensor"), None),
        P(("dp", "tensor"), None),
        *([P()] * 12),
    )
    return jax.shard_map(shards, mesh=mesh, in_specs=in_specs, out_specs=out_specs, check_vma=False)
```

```python
import math

import jax
import jax.numpy as jnp
from jax import lax
from jax.experimental import pallas as pl
from jax.experimental.pallas import tpu as pltpu
from jax.sharding import PartitionSpec as P

HD = 64
EPSILON = 1e-05
MASKED = -1e30
GROUP = 128
BF = jnp.bfloat16
F32 = jnp.float32
AXES = ("dp", "tensor")
GRAD_ROWS = 160


def nn(a, b):
    return lax.dot_general(a, b, (((1,), (0,)), ((), ())), preferred_element_type=F32)


def nt(a, b):
    return lax.dot_general(a, b, (((1,), (1,)), ((), ())), preferred_element_type=F32)


def tn(a, b):
    return lax.dot_general(a, b, (((0,), (0,)), ((), ())), preferred_element_type=F32)


def cdf_of(v):
    return 0.5 * (1.0 + lax.erf(v * (1.0 / math.sqrt(2.0))))


def gelu_slope(v, cdf):
    return cdf + v * (jnp.exp(-0.5 * v * v) * (1.0 / math.sqrt(2.0 * math.pi)))


class Staged:
    def __init__(self, plan, refs, rows_ref, dest, sems):
        self.copies = [[] for _ in range(4)]
        i = 0
        for ref, (slot, entries) in zip(refs, plan):
            n = len(entries)
            step = ref.shape[0] // n
            for j, e in enumerate(entries):
                row = pl.multiple_of(rows_ref[e], 32)
                self.copies[slot].append(
                    pltpu.make_async_copy(
                        ref.at[pl.ds(j * step, step), :],
                        dest.at[slot, pl.ds(row, step), :],
                        sems.at[i],
                    )
                )
                i += 1

    def start(self):
        for slot in self.copies:
            for c in slot:
                c.start()

    def wait(self, slot):
        for c in self.copies[slot]:
            c.wait()


def copies_of(plan):
    return sum(len(entries) for _, entries in plan)


def lane_low(rows):
    return lax.broadcasted_iota(jnp.int32, (rows, GROUP), 1) < HD


def stack_heads(pair):
    low = lane_low(pair.shape[0])
    zero = jnp.zeros_like(pair)
    return jnp.concatenate([jnp.where(low, pair, zero), jnp.where(low, zero, pair)], axis=0)


def swap_halves(v):
    return jnp.concatenate([v[:, HD:], v[:, :HD]], axis=1)


def pack_kernel(q_ref, k_ref, v_ref, o_ref, out, wide):
    n = q_ref.shape[0]
    wide[...] = jnp.zeros_like(wide)
    wide[:, 0:n] = o_ref[...].astype(F32)
    turned = wide[...].T[0:n].astype(BF)
    for i, ref in enumerate((q_ref, k_ref, v_ref)):
        out[:, i * GROUP : (i + 1) * GROUP] = ref[:, 0:GROUP]
    out[:, 3 * GROUP : 4 * GROUP] = jnp.concatenate([q_ref[:, GROUP:], k_ref[:, GROUP:]], axis=1)
    out[:, 4 * GROUP : 5 * GROUP] = jnp.concatenate([v_ref[:, GROUP:], turned[:, GROUP:]], axis=1)
    out[:, 5 * GROUP :] = turned[:, 0:GROUP]


def front_kernel(plan, rows):
    pieces = len(plan)

    def body(rows_ref, info_ref, own_ref, other_ref, *refs):
        a_refs = refs[:pieces]
        (down, dbias, up, ubias, gain, shift) = refs[pieces : pieces + 6]
        outs = refs[pieces + 6 :]
        projs, probs2, probs1 = outs[0:4], outs[4:8], outs[8:12]
        (branch_o, pre_o, mid_o, normed_o, inv_o, w, sems) = outs[12:]
        staged = Staged(plan, a_refs, rows_ref, w, sems)
        staged.start()
        length = info_ref[0]
        half = info_ref[1]
        at = lax.broadcasted_iota(jnp.int32, (1, 2 * rows), 1)
        place = jnp.where(at < rows, at + half * rows, at - rows + (1 - half) * rows)
        visible = place < length
        low = lane_low(rows)

        def softmax(raw):
            s = jnp.where(visible, raw * (1.0 / math.sqrt(HD)), MASKED)
            e = jnp.exp(s - jnp.max(s, axis=1, keepdims=True))
            return (e / jnp.sum(e, axis=1, keepdims=True)).astype(BF)

        branch = jnp.zeros((rows, own_ref.shape[1]), F32)
        for t in range(4):
            staged.wait(t)
            proj = projs[t]
            proj[0:rows, :] = nn(own_ref[...], w[t, :, 0 : 5 * GROUP]).astype(BF)
            proj[rows : 2 * rows, GROUP : 5 * GROUP] = nn(
                other_ref[...], w[t, :, GROUP : 5 * GROUP]
            ).astype(BF)
            proj[rows : 2 * rows, 0:GROUP] = jnp.zeros((rows, GROUP), BF)
            p2 = softmax(nt(stack_heads(proj[0:rows, 0:GROUP]), proj[:, GROUP : 2 * GROUP]))
            probs2[t][...] = p2
            both = nn(p2, proj[:, 2 * GROUP : 3 * GROUP])
            pair = jnp.where(low, both[0:rows], both[rows:])
            qc = swap_halves(proj[0:rows, 3 * GROUP : 4 * GROUP])
            qc = jnp.where(low, jnp.zeros_like(qc), qc)
            p1 = softmax(nt(qc, proj[:, 3 * GROUP : 4 * GROUP]))
            probs1[t][...] = p1
            single = swap_halves(nn(p1, proj[:, 4 * GROUP : 5 * GROUP]))
            single = jnp.where(low, 0.0, single)
            context = jnp.concatenate([single, pair], axis=1).astype(BF)
            branch = branch + nt(context, w[t, :, 4 * GROUP : 6 * GROUP])
        branch_low = branch.astype(BF)
        branch_o[...] = branch_low
        pre = nn(branch_low, down[...]) + dbias[...]
        pre_o[...] = pre
        hidden = (pre * cdf_of(pre)).astype(BF)
        total = own_ref[...].astype(F32) + (branch_low.astype(F32) + nn(hidden, up[...]) + ubias[...])
        center = total - jnp.mean(total, axis=1, keepdims=True)
        inverse = lax.rsqrt(jnp.mean(center * center, axis=1, keepdims=True) + EPSILON)
        normed = center * inverse
        normed_o[...] = normed
        inv_o[...] = inverse
        mid_o[...] = (normed * gain[...] + shift[...]).astype(BF)

    return body


def inner_kernel(plan, rows):
    pieces = len(plan)

    def body(rows_ref, mid_ref, *refs):
        b_refs = refs[:pieces]
        act_o, slope_o, w, sems = refs[pieces:]
        staged = Staged(plan, b_refs, rows_ref, w, sems)
        staged.start()
        for t in range(4):
            staged.wait(t)
            pre = nn(mid_ref[...], w[t])
            cdf = cdf_of(pre)
            act_o[t] = (pre * cdf).astype(BF)
            slope_o[t] = gelu_slope(pre, cdf).astype(BF)

    return body


def norm_back(incoming, normed, inverse, gain):
    gain_grad = jnp.sum(incoming * normed, axis=0, keepdims=True)
    shift_grad = jnp.sum(incoming, axis=0, keepdims=True)
    scaled = incoming * gain
    row_mean = jnp.mean(scaled, axis=1, keepdims=True)
    row_proj = jnp.mean(scaled * normed, axis=1, keepdims=True)
    return inverse * (scaled - row_mean - normed * row_proj), gain_grad, shift_grad


def adapter_back(grads, g, branch_low, pre, hidden, cdf, down, up, gain_grad, shift_grad):
    g_low = g.astype(BF)
    hidden_grad = nt(g_low, up)
    pre_low = (hidden_grad * gelu_slope(pre, cdf)).astype(BF)
    n = pre.shape[1]
    grads[...] = jnp.zeros_like(grads)
    grads[0:n, :] = tn(pre_low, branch_low)
    grads[n : 2 * n, :] = tn(hidden, g_low)
    grads[2 * n : 2 * n + 1, :] = jnp.sum(g, axis=0, keepdims=True)
    grads[2 * n + 1 : 2 * n + 2, :] = gain_grad
    grads[2 * n + 2 : 2 * n + 3, :] = shift_grad
    grads[2 * n + 3 : 2 * n + 4, 0:n] = jnp.sum(pre_low.astype(F32), axis=0, keepdims=True)
    return (g + nt(pre_low, down)).astype(BF)


def middle_kernel(plan, rows):
    pieces = len(plan)

    def body(rows_ref, info_ref, act_ref, slope_ref, mid_ref, upstream, branch_ref, pre_ref, normed_ref, inv_ref, *refs):
        b_refs = refs[:pieces]
        c_refs = refs[pieces : 2 * pieces]
        (fdown, fdbias, fup, fubias, fgain, fshift, adown, aup, again) = refs[2 * pieces : 2 * pieces + 9]
        (out_o, back_o, first_o, keep_o, send_o) = refs[2 * pieces + 9 : 2 * pieces + 14]
        (wb, wc, fgrads, agrads, semb, semc) = refs[2 * pieces + 14 :]
        staged_c = Staged(plan, c_refs, rows_ref, wc, semc)
        staged_b = Staged(plan, b_refs, rows_ref, wb, semb)
        staged_c.start()
        staged_b.start()
        branch = jnp.zeros((rows, mid_ref.shape[1]), F32)
        for t in range(4):
            staged_c.wait(t)
            branch = branch + nt(act_ref[t], wc[t])
        branch_low = branch.astype(BF)
        pre = nn(branch_low, fdown[...]) + fdbias[...]
        cdf = cdf_of(pre)
        hidden = (pre * cdf).astype(BF)
        total = mid_ref[...].astype(F32) + (branch_low.astype(F32) + nn(hidden, fup[...]) + fubias[...])
        center = total - jnp.mean(total, axis=1, keepdims=True)
        inverse = lax.rsqrt(jnp.mean(center * center, axis=1, keepdims=True) + EPSILON)
        normed = center * inverse
        out_o[...] = (normed * fgain[...] + fshift[...]).astype(BF)
        second, gain_grad, shift_grad = norm_back(upstream[...].astype(F32), normed, inverse, fgain[...])
        back = adapter_back(fgrads, second, branch_low, pre, hidden, cdf, fdown[...], fup[...], gain_grad, shift_grad)
        mid_grad = second
        for t in range(4):
            staged_b.wait(t)
            inner_low = (nn(back, wc[t]) * slope_ref[t].astype(F32)).astype(BF)
            mid_grad = mid_grad + nt(inner_low, wb[t])
        normed1 = normed_ref[...]
        first, gain_grad, shift_grad = norm_back(mid_grad, normed1, inv_ref[...], again[...])
        first_o[...] = first
        pre1 = pre_ref[...]
        cdf1 = cdf_of(pre1)
        hidden1 = (pre1 * cdf1).astype(BF)
        back_o[...] = adapter_back(
            agrads, first, branch_ref[...], pre1, hidden1, cdf1, adown[...], aup[...], gain_grad, shift_grad
        )
        is_zero = info_ref[1] == 0
        f_all = fgrads[...]
        a_all = agrads[...]
        keep_o[...] = jnp.where(is_zero, f_all, a_all)
        send_o[...] = jnp.where(is_zero, a_all, f_all).astype(BF)

    return body


def back_kernel(plan, rows, t):
    pieces = len(plan)
    scale = 1.0 / math.sqrt(HD)

    def body(rows_ref, back_ref, proj, probs2, probs1, own_in, sent_in, *refs):
        a_refs = refs[:pieces]
        (own_o, sent_o) = refs[pieces : pieces + 2]
        (w, grad, sems) = refs[pieces + 2 :]
        staged = Staged(plan, a_refs, rows_ref, w, sems)
        staged.start()
        low = lane_low(rows)

        def score_grad(p, dp):
            pf = p.astype(F32)
            inner = jnp.sum(pf * dp, axis=1, keepdims=True)
            return (pf * (dp - inner)).astype(BF)

        staged.wait(0)
        d_context = nn(back_ref[...], w[0, :, 4 * GROUP : 6 * GROUP]).astype(BF)
        d_pair = stack_heads(d_context[:, GROUP:])
        p2 = probs2[...]
        ds = score_grad(p2, nt(d_pair, proj[:, 2 * GROUP : 3 * GROUP]))
        grad[:, 2 * GROUP : 3 * GROUP] = tn(p2, d_pair).astype(BF)
        grad[:, GROUP : 2 * GROUP] = (tn(ds, stack_heads(proj[0:rows, 0:GROUP])) * scale).astype(BF)
        both = nn(ds, proj[:, GROUP : 2 * GROUP]) * scale
        grad[0:rows, 0:GROUP] = jnp.where(low, both[0:rows], both[rows:]).astype(BF)
        d_single = swap_halves(d_context[:, 0:GROUP])
        d_single = jnp.where(low, d_single, jnp.zeros_like(d_single))
        p1 = probs1[...]
        ds1 = score_grad(p1, nt(d_single, proj[:, 4 * GROUP : 5 * GROUP]))
        grad[:, 4 * GROUP : 5 * GROUP] = tn(p1, d_single).astype(BF)
        qc = swap_halves(proj[0:rows, 3 * GROUP : 4 * GROUP])
        qc = jnp.where(low, jnp.zeros_like(qc), qc)
        dk = tn(ds1, qc) * scale
        dq = swap_halves(nn(ds1, proj[:, 3 * GROUP : 4 * GROUP])) * scale
        grad[0:rows, 3 * GROUP : 4 * GROUP] = jnp.where(low, dq, dk[0:rows]).astype(BF)
        grad[rows : 2 * rows, 3 * GROUP : 4 * GROUP] = dk[rows:].astype(BF)
        own_o[...] = own_in[...] + nt(grad[0:rows, :], w[0, :, 0 : 5 * GROUP])
        sent = nt(grad[rows : 2 * rows, GROUP:], w[0, :, GROUP : 5 * GROUP])
        sent_o[...] = (sent_in[...] + sent).astype(sent_o.dtype)

    return body


VM = pl.BlockSpec(memory_space=pltpu.VMEM)
SM = pl.BlockSpec(memory_space=pltpu.SMEM)
ANY = pl.BlockSpec(memory_space=pl.ANY)


def call(body, name, in_specs, outs, scratch, micros):
    return pl.pallas_call(
        body,
        name=name,
        in_specs=in_specs,
        out_specs=[VM] * len(outs),
        out_shape=[jax.ShapeDtypeStruct(s, d) for s, d in outs],
        scratch_shapes=scratch,
        cost_estimate=pl.CostEstimate(flops=int(micros * 1e9), transcendentals=0, bytes_accessed=1 << 20),
        compiler_params=pltpu.CompilerParams(vmem_limit_bytes=60000 * 1024),
    )


def pairs(step):
    out = []
    for d in range(8):
        for t in range(4):
            z, y, x, c = d // 2, d % 2, t // 2, t % 2
            z2, y2, x2, c2 = step(z, y, x, c)
            out.append((d * 4 + t, (z2 * 2 + y2) * 4 + x2 * 2 + c2))
    return out


CORE = pairs(lambda z, y, x, c: (z, y, x, 1 - c))
XDIR = pairs(lambda z, y, x, c: (z, y, 1 - x, c))
YDIR = pairs(lambda z, y, x, c: (z, 1 - y, x, c))
ZDIR = [None] + [pairs(lambda z, y, x, c, k=k: (z ^ k, y, x, c)) for k in (1, 2, 3)]
SPLIT1 = pairs(lambda z, y, x, c: (z, y, 1 - x, c) if c == 0 else (z, 1 - y, x, c))
SPLIT2 = pairs(lambda z, y, x, c: (z, 1 - y, x, c) if c == 0 else (z, y, 1 - x, c))


def pp(v, perm):
    return lax.ppermute(v, AXES, perm)


def fast_plan():
    plan = []
    for rc in range(2):
        plan += [
            (rc, [0, 1, 2, 3]),
            (2 + rc, [0, 1, 2, 3]),
            (rc, [4, 5, 6, 7]),
            (2 + rc, [4, 5]),
            (2 + rc, [6, 7]),
        ]
    return plan


def after(value, *others):
    return lax.optimization_barrier((value, *others))[0]


class Gather:
    def __init__(self, shard):
        self.shard = shard
        self.n = shard.shape[0]

    def depth(self):
        parts = [self.shard] + [pp(self.shard, ZDIR[k]) for k in (1, 2, 3)]
        self.line = jnp.concatenate(parts, axis=0)

    def plane(self):
        self.from_x = pp(self.line, XDIR)
        self.from_y = pp(self.line, YDIR)

    def corner(self):
        self.corner_x = pp(self.from_y[: 2 * self.n], XDIR)
        self.corner_y = pp(self.from_x[2 * self.n :], YDIR)

    def pieces(self):
        mine = [self.line, self.from_x, self.from_y, self.corner_x, self.corner_y]
        return mine + [pp(v, CORE) for v in mine]


class Gathers:
    def __init__(self, a, b, c, small):
        self.a, self.b, self.c = a, b, c = Gather(a), Gather(b), Gather(c)
        a.depth()
        a.line, *self.small = lax.optimization_barrier((a.line, *small))
        a.plane()
        b.shard = after(b.shard, a.line)
        b.depth()
        c.shard = after(c.shard, b.line)
        c.depth()
        a.corner()
        b.line = after(b.line, a.corner_x, a.corner_y)
        b.plane()

    def first(self):
        b, c = self.b, self.c
        b.from_x, b.from_y, *pieces = lax.optimization_barrier((b.from_x, b.from_y, *self.a.pieces()))
        b.corner()
        c.line = after(c.line, b.from_x, b.from_y)
        c.plane()
        return pieces

    def second(self, mid):
        b, c = self.b, self.c
        b.corner_x, b.corner_y, _ = lax.optimization_barrier((b.corner_x, b.corner_y, mid))
        c.from_x, c.from_y, _ = lax.optimization_barrier((c.from_x, c.from_y, mid))
        c.from_x, c.from_y, *pieces = lax.optimization_barrier((c.from_x, c.from_y, *b.pieces()))
        c.corner()
        return pieces

    def third(self, act):
        c = self.c
        c.corner_x, c.corner_y, _ = lax.optimization_barrier((c.corner_x, c.corner_y, act))
        return c.pieces()


def gather_plain(shard):
    n = shard.shape[0]
    whole = lax.all_gather(shard, AXES, axis=0, tiled=False)
    whole = whole.reshape(lax.axis_size("dp"), lax.axis_size("tensor"), n, shard.shape[1])
    return [whole[:, t].reshape(-1, shard.shape[1]) for t in range(lax.axis_size("tensor"))]


def reduce_fast(keep, send, c, x, y, steps):
    first = jnp.where(c == 0, x, y) == 1
    second = jnp.where(c == 0, y, x) == 1
    half = keep + pp(send, CORE).astype(F32)
    n = half.shape[0] // 2
    m = half.shape[1] // 2
    lo, hi = half[:n], half[n:]
    quarter = jnp.where(first, hi, lo) + after(
        pp(jnp.where(first, lo, hi).astype(BF), SPLIT1), steps[0]
    ).astype(F32)
    lo, hi = quarter[:, :m], quarter[:, m:]
    part = jnp.where(second, hi, lo) + after(
        pp(jnp.where(second, lo, hi).astype(BF), SPLIT2), steps[1]
    ).astype(F32)
    low = part.astype(BF)
    others = [after(pp(low, ZDIR[k]), steps[2]).astype(F32) for k in (1, 2, 3)]
    part = ((low.astype(F32) + others[0]) + (others[1] + others[2])).astype(BF)
    other = after(pp(part, SPLIT2), steps[3])
    quarter = jnp.where(second, jnp.concatenate([other, part], 1), jnp.concatenate([part, other], 1))
    other = pp(quarter, SPLIT1)
    half = jnp.where(first, jnp.concatenate([other, quarter], 0), jnp.concatenate([quarter, other], 0))
    other = pp(half, CORE)
    return jnp.where(c == 0, half, other).astype(F32), jnp.where(c == 0, other, half).astype(F32)


def shards(
    tokens,
    lengths,
    query_weight,
    key_weight,
    value_weight,
    output_weight,
    inner_weight,
    outer_weight,
    attn_down,
    attn_down_bias,
    attn_up,
    attn_up_bias,
    attn_norm_gain,
    attn_norm_bias,
    feed_down,
    feed_down_bias,
    feed_up,
    feed_up_bias,
    feed_norm_gain,
    feed_norm_bias,
    upstream,
):
    dp_size, t_size = lax.axis_size("dp"), lax.axis_size("tensor")
    fast = dp_size == 8 and t_size == 4
    d = lax.axis_index("dp")
    t = lax.axis_index("tensor")
    rows, width = tokens.shape
    units = inner_weight.shape[1]
    n_adapt = attn_down.shape[1]

    partner = [(i * t_size + j, i * t_size + (j ^ 1)) for i in range(dp_size) for j in range(t_size)]
    other_tokens = pp(tokens, partner)

    pack_a = call(
        pack_kernel,
        "pack",
        [VM] * 4,
        [((query_weight.shape[0], 6 * GROUP), BF)],
        [pltpu.VMEM((3 * HD, GROUP), F32)],
        1,
    )(query_weight, key_weight, value_weight, output_weight)[0]
    pack_c = outer_weight.T
    if fast:
        plan = fast_plan()
        z, y = d // 2, d % 2
        table = jnp.stack([((z ^ rz) * 2 + (y ^ ry)) * (width // 8) for ry in range(2) for rz in range(4)])
    else:
        plan = [(s, [0]) for s in range(4)]
        a_pieces, b_pieces, c_pieces = (gather_plain(s) for s in (pack_a, inner_weight, pack_c))
        table = jnp.zeros((8,), jnp.int32)
    table = table.astype(jnp.int32)
    count = copies_of(plan)
    half = t % 2
    info = jnp.stack([lengths[t // 2], half]).astype(jnp.int32)
    vectors = (
        attn_down_bias,
        attn_up_bias,
        attn_norm_gain,
        attn_norm_bias,
        feed_down_bias,
        feed_up_bias,
        feed_norm_gain,
        feed_norm_bias,
    )
    small = [table, info, attn_down, attn_up, feed_down, feed_up] + [v.reshape(1, -1) for v in vectors]
    if fast:
        gathers = Gathers(pack_a, inner_weight, pack_c, small)
        small = gathers.small
        a_pieces = gathers.first()
    (table, info, attn_down, attn_up, feed_down, feed_up, a_dbias, a_ubias, a_gain, a_shift, f_dbias, f_ubias, f_gain, f_shift) = small

    w_shape = pltpu.VMEM((4, width, width), BF)
    sem_shape = pltpu.SemaphoreType.DMA((count,))
    n_p = len(plan)

    *heads, branch, pre, mid, normed, inv = call(
        front_kernel(plan, rows),
        "front",
        [SM, SM, VM, VM] + [ANY] * n_p + [VM] * 6,
        [
            *([((2 * rows, 5 * GROUP), BF)] * 4),
            *([((2 * rows, 2 * rows), BF)] * 4),
            *([((rows, 2 * rows), BF)] * 4),
            ((rows, width), BF),
            ((rows, n_adapt), F32),
            ((rows, width), BF),
            ((rows, width), F32),
            ((rows, 1), F32),
        ],
        [w_shape, sem_shape],
        12,
    )(
        table,
        info,
        tokens,
        other_tokens,
        *a_pieces,
        attn_down,
        a_dbias,
        attn_up,
        a_ubias,
        a_gain,
        a_shift,
    )

    if fast:
        b_pieces = gathers.second(mid)
    act, slope = call(
        inner_kernel(plan, rows),
        "inner",
        [SM, VM] + [ANY] * n_p,
        [((4, rows, units), BF), ((4, rows, units), BF)],
        [w_shape, sem_shape],
        7,
    )(table, mid, *b_pieces)

    if fast:
        c_pieces = gathers.third(act)
    layer_out, attn_back, first, keep, send = call(
        middle_kernel(plan, rows),
        "middle",
        [SM, SM] + [VM] * 8 + [ANY] * (2 * n_p) + [VM] * 9,
        [
            ((rows, width), BF),
            ((rows, width), BF),
            ((rows, width), F32),
            ((GRAD_ROWS, width), F32),
            ((GRAD_ROWS, width), BF),
        ],
        [
            w_shape,
            w_shape,
            pltpu.VMEM((GRAD_ROWS, width), F32),
            pltpu.VMEM((GRAD_ROWS, width), F32),
            sem_shape,
            sem_shape,
        ],
        15,
    )(
        table,
        info,
        act,
        slope,
        mid,
        upstream,
        branch,
        pre,
        normed,
        inv,
        *b_pieces,
        *c_pieces,
        feed_down,
        f_dbias,
        feed_up,
        f_ubias,
        f_gain,
        f_shift,
        attn_down,
        attn_up,
        a_gain,
    )

    own, sent, steps = first, jnp.zeros((rows, width), F32), []
    for slot in range(4):
        chosen = [i for i, (at, _) in enumerate(plan) if at == slot]
        own_plan = [(0, plan[i][1]) for i in chosen]
        own, sent = call(
            back_kernel(own_plan, rows, slot),
            f"back{slot}",
            [SM] + [VM] * 6 + [ANY] * len(chosen),
            [((rows, width), F32), ((rows, width), F32 if slot < 3 else BF)],
            [
                pltpu.VMEM((1, width, width), BF),
                pltpu.VMEM((2 * rows, 5 * GROUP), BF),
                pltpu.SemaphoreType.DMA((copies_of(own_plan),)),
            ],
            4,
        )(
            table,
            attn_back,
            heads[slot],
            heads[4 + slot],
            heads[8 + slot],
            own,
            sent,
            *[a_pieces[i] for i in chosen],
        )
        steps.append(own)
    tokens_grad = (own + pp(sent, partner).astype(F32)).astype(BF)

    if fast:
        feed_g, attn_g = reduce_fast(keep, send, half, t // 2, d % 2, steps)
    else:
        is_zero = half == 0
        sent32 = send.astype(F32)
        feed_g = lax.psum(jnp.where(is_zero, keep, sent32), AXES)
        attn_g = lax.psum(jnp.where(is_zero, sent32, keep), AXES)
    grad_scale = 1.0 / math.sqrt(rows * dp_size * t_size)

    def outputs(g):
        g = g * grad_scale
        n = n_adapt
        return [
            g[:n].T,
            g[2 * n + 3, :n],
            g[n : 2 * n],
            g[2 * n],
            g[2 * n + 1],
            g[2 * n + 2],
        ]

    return (layer_out, tokens_grad, *outputs(attn_g), *outputs(feed_g))


def solution(mesh):
    in_specs = (
        P(("dp", "tensor"), None),
        P("dp"),
        P("dp", "tensor"),
        P("dp", "tensor"),
        P("dp", "tensor"),
        P("tensor", "dp"),
        P("dp", "tensor"),
        P("tensor", "dp"),
        *([P()] * 12),
        P(("dp", "tensor"), None),
    )
    out_specs = (
        P(("dp", "tensor"), None),
        P(("dp", "tensor"), None),
        *([P()] * 12),
    )
    return jax.shard_map(shards, mesh=mesh, in_specs=in_specs, out_specs=out_specs, check_vma=False)
```

```python
import math

import jax
import jax.numpy as jnp
from jax import lax
from jax.experimental import pallas as pl
from jax.experimental.pallas import tpu as pltpu
from jax.sharding import PartitionSpec as P

HD = 64
EPSILON = 1e-05
MASKED = -1e30
GROUP = 128
BF = jnp.bfloat16
F32 = jnp.float32
AXES = ("dp", "tensor")
GRAD_ROWS = 160


def nn(a, b):
    return lax.dot_general(a, b, (((1,), (0,)), ((), ())), preferred_element_type=F32)


def nt(a, b):
    return lax.dot_general(a, b, (((1,), (1,)), ((), ())), preferred_element_type=F32)


def tn(a, b):
    return lax.dot_general(a, b, (((0,), (0,)), ((), ())), preferred_element_type=F32)


def cdf_of(v):
    return 0.5 * (1.0 + lax.erf(v * (1.0 / math.sqrt(2.0))))


def gelu_slope(v, cdf):
    return cdf + v * (jnp.exp(-0.5 * v * v) * (1.0 / math.sqrt(2.0 * math.pi)))


class Staged:
    def __init__(self, plan, refs, rows_ref, dest, sems):
        self.copies = [[] for _ in range(4)]
        i = 0
        for ref, (slot, entries) in zip(refs, plan):
            n = len(entries)
            step = ref.shape[0] // n
            for j, e in enumerate(entries):
                row = pl.multiple_of(rows_ref[e], 32)
                self.copies[slot].append(
                    pltpu.make_async_copy(
                        ref.at[pl.ds(j * step, step), :],
                        dest.at[slot, pl.ds(row, step), :],
                        sems.at[i],
                    )
                )
                i += 1

    def start(self):
        for slot in self.copies:
            for c in slot:
                c.start()

    def wait(self, slot):
        for c in self.copies[slot]:
            c.wait()


def copies_of(plan):
    return sum(len(entries) for _, entries in plan)


def lane_low(rows):
    return lax.broadcasted_iota(jnp.int32, (rows, GROUP), 1) < HD


def stack_heads(pair):
    low = lane_low(pair.shape[0])
    zero = jnp.zeros_like(pair)
    return jnp.concatenate([jnp.where(low, pair, zero), jnp.where(low, zero, pair)], axis=0)


def swap_halves(v):
    return jnp.concatenate([v[:, HD:], v[:, :HD]], axis=1)


def pack_kernel(q_ref, k_ref, v_ref, o_ref, out, wide):
    n = q_ref.shape[0]
    wide[...] = jnp.zeros_like(wide)
    wide[:, 0:n] = o_ref[...].astype(F32)
    turned = wide[...].T[0:n].astype(BF)
    for i, ref in enumerate((q_ref, k_ref, v_ref)):
        out[:, i * GROUP : (i + 1) * GROUP] = ref[:, 0:GROUP]
    out[:, 3 * GROUP : 4 * GROUP] = jnp.concatenate([q_ref[:, GROUP:], k_ref[:, GROUP:]], axis=1)
    out[:, 4 * GROUP : 5 * GROUP] = jnp.concatenate([v_ref[:, GROUP:], turned[:, GROUP:]], axis=1)
    out[:, 5 * GROUP :] = turned[:, 0:GROUP]


def front_kernel(plan, rows):
    pieces = len(plan)

    def body(rows_ref, info_ref, own_ref, other_ref, *refs):
        a_refs = refs[:pieces]
        (down, dbias, up, ubias, gain, shift) = refs[pieces : pieces + 6]
        outs = refs[pieces + 6 :]
        projs, probs2, probs1 = outs[0:4], outs[4:8], outs[8:12]
        (branch_o, pre_o, mid_o, normed_o, inv_o, w, sems) = outs[12:]
        staged = Staged(plan, a_refs, rows_ref, w, sems)
        staged.start()
        length = info_ref[0]
        half = info_ref[1]
        at = lax.broadcasted_iota(jnp.int32, (1, 2 * rows), 1)
        place = jnp.where(at < rows, at + half * rows, at - rows + (1 - half) * rows)
        visible = place < length
        low = lane_low(rows)

        def softmax(raw):
            s = jnp.where(visible, raw * (1.0 / math.sqrt(HD)), MASKED)
            e = jnp.exp(s - jnp.max(s, axis=1, keepdims=True))
            return (e / jnp.sum(e, axis=1, keepdims=True)).astype(BF)

        branch = jnp.zeros((rows, own_ref.shape[1]), F32)
        for t in range(4):
            staged.wait(t)
            proj = projs[t]
            proj[0:rows, :] = nn(own_ref[...], w[t, :, 0 : 5 * GROUP]).astype(BF)
            proj[rows : 2 * rows, GROUP : 5 * GROUP] = nn(
                other_ref[...], w[t, :, GROUP : 5 * GROUP]
            ).astype(BF)
            proj[rows : 2 * rows, 0:GROUP] = jnp.zeros((rows, GROUP), BF)
            p2 = softmax(nt(stack_heads(proj[0:rows, 0:GROUP]), proj[:, GROUP : 2 * GROUP]))
            probs2[t][...] = p2
            both = nn(p2, proj[:, 2 * GROUP : 3 * GROUP])
            pair = jnp.where(low, both[0:rows], both[rows:])
            qc = swap_halves(proj[0:rows, 3 * GROUP : 4 * GROUP])
            qc = jnp.where(low, jnp.zeros_like(qc), qc)
            p1 = softmax(nt(qc, proj[:, 3 * GROUP : 4 * GROUP]))
            probs1[t][...] = p1
            single = swap_halves(nn(p1, proj[:, 4 * GROUP : 5 * GROUP]))
            single = jnp.where(low, 0.0, single)
            context = jnp.concatenate([single, pair], axis=1).astype(BF)
            branch = branch + nt(context, w[t, :, 4 * GROUP : 6 * GROUP])
        branch_low = branch.astype(BF)
        branch_o[...] = branch_low
        pre = nn(branch_low, down[...]) + dbias[...]
        pre_o[...] = pre
        hidden = (pre * cdf_of(pre)).astype(BF)
        total = own_ref[...].astype(F32) + (branch_low.astype(F32) + nn(hidden, up[...]) + ubias[...])
        center = total - jnp.mean(total, axis=1, keepdims=True)
        inverse = lax.rsqrt(jnp.mean(center * center, axis=1, keepdims=True) + EPSILON)
        normed = center * inverse
        normed_o[...] = normed
        inv_o[...] = inverse
        mid_o[...] = (normed * gain[...] + shift[...]).astype(BF)

    return body


def inner_kernel(plan, rows):
    pieces = len(plan)

    def body(rows_ref, mid_ref, *refs):
        b_refs = refs[:pieces]
        act_o, slope_o, w, sems = refs[pieces:]
        staged = Staged(plan, b_refs, rows_ref, w, sems)
        staged.start()
        for t in range(4):
            staged.wait(t)
            pre = nn(mid_ref[...], w[t])
            cdf = cdf_of(pre)
            act_o[t] = (pre * cdf).astype(BF)
            slope_o[t] = gelu_slope(pre, cdf).astype(BF)

    return body


def norm_back(incoming, normed, inverse, gain):
    gain_grad = jnp.sum(incoming * normed, axis=0, keepdims=True)
    shift_grad = jnp.sum(incoming, axis=0, keepdims=True)
    scaled = incoming * gain
    row_mean = jnp.mean(scaled, axis=1, keepdims=True)
    row_proj = jnp.mean(scaled * normed, axis=1, keepdims=True)
    return inverse * (scaled - row_mean - normed * row_proj), gain_grad, shift_grad


def adapter_back(grads, g, branch_low, pre, hidden, cdf, down, up, gain_grad, shift_grad):
    g_low = g.astype(BF)
    hidden_grad = nt(g_low, up)
    pre_low = (hidden_grad * gelu_slope(pre, cdf)).astype(BF)
    n = pre.shape[1]
    grads[...] = jnp.zeros_like(grads)
    grads[0:n, :] = tn(pre_low, branch_low)
    grads[n : 2 * n, :] = tn(hidden, g_low)
    grads[2 * n : 2 * n + 1, :] = jnp.sum(g, axis=0, keepdims=True)
    grads[2 * n + 1 : 2 * n + 2, :] = gain_grad
    grads[2 * n + 2 : 2 * n + 3, :] = shift_grad
    grads[2 * n + 3 : 2 * n + 4, 0:n] = jnp.sum(pre_low.astype(F32), axis=0, keepdims=True)
    return (g + nt(pre_low, down)).astype(BF)


def middle_kernel(plan, rows):
    pieces = len(plan)

    def body(rows_ref, info_ref, act_ref, slope_ref, mid_ref, upstream, branch_ref, pre_ref, normed_ref, inv_ref, *refs):
        b_refs = refs[:pieces]
        c_refs = refs[pieces : 2 * pieces]
        (fdown, fdbias, fup, fubias, fgain, fshift, adown, aup, again) = refs[2 * pieces : 2 * pieces + 9]
        (out_o, back_o, first_o, keep_o, send_o) = refs[2 * pieces + 9 : 2 * pieces + 14]
        (wb, wc, fgrads, agrads, semb, semc) = refs[2 * pieces + 14 :]
        staged_c = Staged(plan, c_refs, rows_ref, wc, semc)
        staged_b = Staged(plan, b_refs, rows_ref, wb, semb)
        staged_c.start()
        staged_b.start()
        branch = jnp.zeros((rows, mid_ref.shape[1]), F32)
        for t in range(4):
            staged_c.wait(t)
            branch = branch + nt(act_ref[t], wc[t])
        branch_low = branch.astype(BF)
        pre = nn(branch_low, fdown[...]) + fdbias[...]
        cdf = cdf_of(pre)
        hidden = (pre * cdf).astype(BF)
        total = mid_ref[...].astype(F32) + (branch_low.astype(F32) + nn(hidden, fup[...]) + fubias[...])
        center = total - jnp.mean(total, axis=1, keepdims=True)
        inverse = lax.rsqrt(jnp.mean(center * center, axis=1, keepdims=True) + EPSILON)
        normed = center * inverse
        out_o[...] = (normed * fgain[...] + fshift[...]).astype(BF)
        second, gain_grad, shift_grad = norm_back(upstream[...].astype(F32), normed, inverse, fgain[...])
        back = adapter_back(fgrads, second, branch_low, pre, hidden, cdf, fdown[...], fup[...], gain_grad, shift_grad)
        mid_grad = second
        for t in range(4):
            staged_b.wait(t)
            inner_low = (nn(back, wc[t]) * slope_ref[t].astype(F32)).astype(BF)
            mid_grad = mid_grad + nt(inner_low, wb[t])
        normed1 = normed_ref[...]
        first, gain_grad, shift_grad = norm_back(mid_grad, normed1, inv_ref[...], again[...])
        first_o[...] = first
        pre1 = pre_ref[...]
        cdf1 = cdf_of(pre1)
        hidden1 = (pre1 * cdf1).astype(BF)
        back_o[...] = adapter_back(
            agrads, first, branch_ref[...], pre1, hidden1, cdf1, adown[...], aup[...], gain_grad, shift_grad
        )
        is_zero = info_ref[1] == 0
        f_all = fgrads[...]
        a_all = agrads[...]
        keep_o[...] = jnp.where(is_zero, f_all, a_all)
        send_o[...] = jnp.where(is_zero, a_all, f_all).astype(BF)

    return body


def back_kernel(plan, rows, t):
    pieces = len(plan)
    scale = 1.0 / math.sqrt(HD)

    def body(rows_ref, back_ref, proj, probs2, probs1, own_in, sent_in, *refs):
        a_refs = refs[:pieces]
        (own_o, sent_o) = refs[pieces : pieces + 2]
        (w, grad, sems) = refs[pieces + 2 :]
        staged = Staged(plan, a_refs, rows_ref, w, sems)
        staged.start()
        low = lane_low(rows)

        def score_grad(p, dp):
            pf = p.astype(F32)
            inner = jnp.sum(pf * dp, axis=1, keepdims=True)
            return (pf * (dp - inner)).astype(BF)

        staged.wait(0)
        d_context = nn(back_ref[...], w[0, :, 4 * GROUP : 6 * GROUP]).astype(BF)
        d_pair = stack_heads(d_context[:, GROUP:])
        p2 = probs2[...]
        ds = score_grad(p2, nt(d_pair, proj[:, 2 * GROUP : 3 * GROUP]))
        grad[:, 2 * GROUP : 3 * GROUP] = tn(p2, d_pair).astype(BF)
        grad[:, GROUP : 2 * GROUP] = (tn(ds, stack_heads(proj[0:rows, 0:GROUP])) * scale).astype(BF)
        both = nn(ds, proj[:, GROUP : 2 * GROUP]) * scale
        grad[0:rows, 0:GROUP] = jnp.where(low, both[0:rows], both[rows:]).astype(BF)
        d_single = swap_halves(d_context[:, 0:GROUP])
        d_single = jnp.where(low, d_single, jnp.zeros_like(d_single))
        p1 = probs1[...]
        ds1 = score_grad(p1, nt(d_single, proj[:, 4 * GROUP : 5 * GROUP]))
        grad[:, 4 * GROUP : 5 * GROUP] = tn(p1, d_single).astype(BF)
        qc = swap_halves(proj[0:rows, 3 * GROUP : 4 * GROUP])
        qc = jnp.where(low, jnp.zeros_like(qc), qc)
        dk = tn(ds1, qc) * scale
        dq = swap_halves(nn(ds1, proj[:, 3 * GROUP : 4 * GROUP])) * scale
        grad[0:rows, 3 * GROUP : 4 * GROUP] = jnp.where(low, dq, dk[0:rows]).astype(BF)
        grad[rows : 2 * rows, 3 * GROUP : 4 * GROUP] = dk[rows:].astype(BF)
        own_o[...] = own_in[...] + nt(grad[0:rows, :], w[0, :, 0 : 5 * GROUP])
        sent = nt(grad[rows : 2 * rows, GROUP:], w[0, :, GROUP : 5 * GROUP])
        sent_o[...] = (sent_in[...] + sent).astype(sent_o.dtype)

    return body


VM = pl.BlockSpec(memory_space=pltpu.VMEM)
SM = pl.BlockSpec(memory_space=pltpu.SMEM)
ANY = pl.BlockSpec(memory_space=pl.ANY)


def call(body, name, in_specs, outs, scratch, micros):
    return pl.pallas_call(
        body,
        name=name,
        in_specs=in_specs,
        out_specs=[VM] * len(outs),
        out_shape=[jax.ShapeDtypeStruct(s, d) for s, d in outs],
        scratch_shapes=scratch,
        cost_estimate=pl.CostEstimate(flops=int(micros * 1e9), transcendentals=0, bytes_accessed=1 << 20),
        compiler_params=pltpu.CompilerParams(vmem_limit_bytes=60000 * 1024),
    )


def pairs(step):
    out = []
    for d in range(8):
        for t in range(4):
            z, y, x, c = d // 2, d % 2, t // 2, t % 2
            z2, y2, x2, c2 = step(z, y, x, c)
            out.append((d * 4 + t, (z2 * 2 + y2) * 4 + x2 * 2 + c2))
    return out


CORE = pairs(lambda z, y, x, c: (z, y, x, 1 - c))
XDIR = pairs(lambda z, y, x, c: (z, y, 1 - x, c))
YDIR = pairs(lambda z, y, x, c: (z, 1 - y, x, c))
ZDIR = [None] + [pairs(lambda z, y, x, c, k=k: (z ^ k, y, x, c)) for k in (1, 2, 3)]
SPLIT1 = pairs(lambda z, y, x, c: (z, y, 1 - x, c) if c == 0 else (z, 1 - y, x, c))
SPLIT2 = pairs(lambda z, y, x, c: (z, 1 - y, x, c) if c == 0 else (z, y, 1 - x, c))


def pp(v, perm):
    return lax.ppermute(v, AXES, perm)


def fast_plan():
    plan = []
    for rc in range(2):
        plan += [
            (rc, [0, 1, 2, 3]),
            (2 + rc, [0, 1, 2, 3]),
            (rc, [4, 5, 6, 7]),
            (2 + rc, [4, 5]),
            (2 + rc, [6, 7]),
        ]
    return plan


def after(value, *others):
    return lax.optimization_barrier((value, *others))[0]


class Gather:
    def __init__(self, shard):
        self.shard = shard
        self.n = shard.shape[0]

    def depth(self):
        parts = [self.shard] + [pp(self.shard, ZDIR[k]) for k in (1, 2, 3)]
        self.line = jnp.concatenate(parts, axis=0)

    def plane(self):
        self.from_x = pp(self.line, XDIR)
        self.from_y = pp(self.line, YDIR)

    def corner(self):
        self.corner_x = pp(self.from_y[: 2 * self.n], XDIR)
        self.corner_y = pp(self.from_x[2 * self.n :], YDIR)

    def pieces(self):
        mine = [self.line, self.from_x, self.from_y, self.corner_x, self.corner_y]
        copied = getattr(self, "copied", {})
        return mine + [copied[i] if i in copied else pp(v, CORE) for i, v in enumerate(mine)]


class Gathers:
    def __init__(self, a, b, c, small):
        self.a, self.b, self.c = a, b, c = Gather(a), Gather(b), Gather(c)
        a.depth()
        a.line, *self.small = lax.optimization_barrier((a.line, *small))
        a.plane()
        b.shard = after(b.shard, a.line)
        b.depth()
        c.shard = after(c.shard, b.line)
        c.depth()
        a.corner()
        b.line, c.line, _, _ = lax.optimization_barrier((b.line, c.line, a.corner_x, a.corner_y))
        b.plane()

    def first(self):
        b, c = self.b, self.c
        b.from_x, b.from_y, *pieces = lax.optimization_barrier((b.from_x, b.from_y, *self.a.pieces()))
        b.corner()
        b.copied = {1: pp(b.from_x, CORE)}
        c.line = after(c.line, b.copied[1])
        c.plane()
        return pieces

    def second(self, mid):
        b, c = self.b, self.c
        b.corner_x, b.corner_y, _ = lax.optimization_barrier((b.corner_x, b.corner_y, mid))
        c.from_x, c.from_y, _ = lax.optimization_barrier((c.from_x, c.from_y, mid))
        c.from_x, c.from_y, *pieces = lax.optimization_barrier((c.from_x, c.from_y, *b.pieces()))
        c.corner()
        return pieces

    def third(self, act):
        c = self.c
        c.corner_x, c.corner_y, _ = lax.optimization_barrier((c.corner_x, c.corner_y, act))
        return c.pieces()


def gather_plain(shard):
    n = shard.shape[0]
    whole = lax.all_gather(shard, AXES, axis=0, tiled=False)
    whole = whole.reshape(lax.axis_size("dp"), lax.axis_size("tensor"), n, shard.shape[1])
    return [whole[:, t].reshape(-1, shard.shape[1]) for t in range(lax.axis_size("tensor"))]


def reduce_fast(keep, send, c, x, y, steps):
    first = jnp.where(c == 0, x, y) == 1
    second = jnp.where(c == 0, y, x) == 1
    half = keep + pp(send, CORE).astype(F32)
    n = half.shape[0] // 2
    m = half.shape[1] // 2
    lo, hi = half[:n], half[n:]
    quarter = jnp.where(first, hi, lo) + after(
        pp(jnp.where(first, lo, hi).astype(BF), SPLIT1), steps[0]
    ).astype(F32)
    lo, hi = quarter[:, :m], quarter[:, m:]
    part = jnp.where(second, hi, lo) + after(
        pp(jnp.where(second, lo, hi).astype(BF), SPLIT2), steps[1]
    ).astype(F32)
    low = part.astype(BF)
    others = [after(pp(low, ZDIR[k]), steps[2]).astype(F32) for k in (1, 2, 3)]
    part = ((low.astype(F32) + others[0]) + (others[1] + others[2])).astype(BF)
    other = after(pp(part, SPLIT2), steps[3])
    quarter = jnp.where(second, jnp.concatenate([other, part], 1), jnp.concatenate([part, other], 1))
    other = pp(quarter, SPLIT1)
    half = jnp.where(first, jnp.concatenate([other, quarter], 0), jnp.concatenate([quarter, other], 0))
    other = pp(half, CORE)
    return jnp.where(c == 0, half, other).astype(F32), jnp.where(c == 0, other, half).astype(F32)


def shards(
    tokens,
    lengths,
    query_weight,
    key_weight,
    value_weight,
    output_weight,
    inner_weight,
    outer_weight,
    attn_down,
    attn_down_bias,
    attn_up,
    attn_up_bias,
    attn_norm_gain,
    attn_norm_bias,
    feed_down,
    feed_down_bias,
    feed_up,
    feed_up_bias,
    feed_norm_gain,
    feed_norm_bias,
    upstream,
):
    dp_size, t_size = lax.axis_size("dp"), lax.axis_size("tensor")
    fast = dp_size == 8 and t_size == 4
    d = lax.axis_index("dp")
    t = lax.axis_index("tensor")
    rows, width = tokens.shape
    units = inner_weight.shape[1]
    n_adapt = attn_down.shape[1]

    partner = [(i * t_size + j, i * t_size + (j ^ 1)) for i in range(dp_size) for j in range(t_size)]
    other_tokens = pp(tokens, partner)

    pack_a = call(
        pack_kernel,
        "pack",
        [VM] * 4,
        [((query_weight.shape[0], 6 * GROUP), BF)],
        [pltpu.VMEM((3 * HD, GROUP), F32)],
        1,
    )(query_weight, key_weight, value_weight, output_weight)[0]
    pack_c = outer_weight.T
    if fast:
        plan = fast_plan()
        z, y = d // 2, d % 2
        table = jnp.stack([((z ^ rz) * 2 + (y ^ ry)) * (width // 8) for ry in range(2) for rz in range(4)])
    else:
        plan = [(s, [0]) for s in range(4)]
        a_pieces, b_pieces, c_pieces = (gather_plain(s) for s in (pack_a, inner_weight, pack_c))
        table = jnp.zeros((8,), jnp.int32)
    table = table.astype(jnp.int32)
    count = copies_of(plan)
    half = t % 2
    info = jnp.stack([lengths[t // 2], half]).astype(jnp.int32)
    vectors = (
        attn_down_bias,
        attn_up_bias,
        attn_norm_gain,
        attn_norm_bias,
        feed_down_bias,
        feed_up_bias,
        feed_norm_gain,
        feed_norm_bias,
    )
    small = [table, info, attn_down, attn_up, feed_down, feed_up] + [v.reshape(1, -1) for v in vectors]
    if fast:
        gathers = Gathers(pack_a, inner_weight, pack_c, small)
        small = gathers.small
        a_pieces = gathers.first()
    (table, info, attn_down, attn_up, feed_down, feed_up, a_dbias, a_ubias, a_gain, a_shift, f_dbias, f_ubias, f_gain, f_shift) = small

    w_shape = pltpu.VMEM((4, width, width), BF)
    sem_shape = pltpu.SemaphoreType.DMA((count,))
    n_p = len(plan)

    *heads, branch, pre, mid, normed, inv = call(
        front_kernel(plan, rows),
        "front",
        [SM, SM, VM, VM] + [ANY] * n_p + [VM] * 6,
        [
            *([((2 * rows, 5 * GROUP), BF)] * 4),
            *([((2 * rows, 2 * rows), BF)] * 4),
            *([((rows, 2 * rows), BF)] * 4),
            ((rows, width), BF),
            ((rows, n_adapt), F32),
            ((rows, width), BF),
            ((rows, width), F32),
            ((rows, 1), F32),
        ],
        [w_shape, sem_shape],
        12,
    )(
        table,
        info,
        tokens,
        other_tokens,
        *a_pieces,
        attn_down,
        a_dbias,
        attn_up,
        a_ubias,
        a_gain,
        a_shift,
    )

    if fast:
        b_pieces = gathers.second(mid)
    act, slope = call(
        inner_kernel(plan, rows),
        "inner",
        [SM, VM] + [ANY] * n_p,
        [((4, rows, units), BF), ((4, rows, units), BF)],
        [w_shape, sem_shape],
        7,
    )(table, mid, *b_pieces)

    if fast:
        c_pieces = gathers.third(act)
    layer_out, attn_back, first, keep, send = call(
        middle_kernel(plan, rows),
        "middle",
        [SM, SM] + [VM] * 8 + [ANY] * (2 * n_p) + [VM] * 9,
        [
            ((rows, width), BF),
            ((rows, width), BF),
            ((rows, width), F32),
            ((GRAD_ROWS, width), F32),
            ((GRAD_ROWS, width), BF),
        ],
        [
            w_shape,
            w_shape,
            pltpu.VMEM((GRAD_ROWS, width), F32),
            pltpu.VMEM((GRAD_ROWS, width), F32),
            sem_shape,
            sem_shape,
        ],
        15,
    )(
        table,
        info,
        act,
        slope,
        mid,
        upstream,
        branch,
        pre,
        normed,
        inv,
        *b_pieces,
        *c_pieces,
        feed_down,
        f_dbias,
        feed_up,
        f_ubias,
        f_gain,
        f_shift,
        attn_down,
        attn_up,
        a_gain,
    )

    own, sent, steps = first, jnp.zeros((rows, width), F32), []
    for slot in range(4):
        chosen = [i for i, (at, _) in enumerate(plan) if at == slot]
        own_plan = [(0, plan[i][1]) for i in chosen]
        own, sent = call(
            back_kernel(own_plan, rows, slot),
            f"back{slot}",
            [SM] + [VM] * 6 + [ANY] * len(chosen),
            [((rows, width), F32), ((rows, width), F32 if slot < 3 else BF)],
            [
                pltpu.VMEM((1, width, width), BF),
                pltpu.VMEM((2 * rows, 5 * GROUP), BF),
                pltpu.SemaphoreType.DMA((copies_of(own_plan),)),
            ],
            4,
        )(
            table,
            attn_back,
            heads[slot],
            heads[4 + slot],
            heads[8 + slot],
            own,
            sent,
            *[a_pieces[i] for i in chosen],
        )
        steps.append(own)
    tokens_grad = (own + pp(sent, partner).astype(F32)).astype(BF)

    if fast:
        feed_g, attn_g = reduce_fast(keep, send, half, t // 2, d % 2, steps)
    else:
        is_zero = half == 0
        sent32 = send.astype(F32)
        feed_g = lax.psum(jnp.where(is_zero, keep, sent32), AXES)
        attn_g = lax.psum(jnp.where(is_zero, sent32, keep), AXES)
    grad_scale = 1.0 / math.sqrt(rows * dp_size * t_size)

    def outputs(g):
        g = g * grad_scale
        n = n_adapt
        return [
            g[:n].T,
            g[2 * n + 3, :n],
            g[n : 2 * n],
            g[2 * n],
            g[2 * n + 1],
            g[2 * n + 2],
        ]

    return (layer_out, tokens_grad, *outputs(attn_g), *outputs(feed_g))


def solution(mesh):
    in_specs = (
        P(("dp", "tensor"), None),
        P("dp"),
        P("dp", "tensor"),
        P("dp", "tensor"),
        P("dp", "tensor"),
        P("tensor", "dp"),
        P("dp", "tensor"),
        P("tensor", "dp"),
        *([P()] * 12),
        P(("dp", "tensor"), None),
    )
    out_specs = (
        P(("dp", "tensor"), None),
        P(("dp", "tensor"), None),
        *([P()] * 12),
    )
    return jax.shard_map(shards, mesh=mesh, in_specs=in_specs, out_specs=out_specs, check_vma=False)
```
